32 devices in a mesh: tile: 16 (over z, y, x), pos: 2 (over core).
Axes of the slice: x: 2, y: 2, z: 4, core: 2. Of those that a mesh axis runs over, the one named last changes fastest.
Arguments:
- object_field: float32 [2, 2048, 1024], P(None, 'tile'), may hold values from -10 to 10
- probe_field: float32 [2, 128, 128], replicated, may hold values from -4 to 4
- amplitudes: float32 [16, 2, 32, 128, 128], P('tile', 'pos'), may hold values from 0 to 2
- scan_rows: int32 [16, 2, 32], P('tile', 'pos'), may hold values from 0 to 127
- scan_cols: int32 [16, 2, 32], P('tile', 'pos'), may hold values from 0 to 1023
- live_count: int32 [16, 2], P('tile', 'pos'), may hold values from 8 to 32, as said below
Outputs:
- object_out: float32 [2, 2048, 1024], P(None, 'tile')
- probe_out: float32 [2, 128, 128], replicated
The draws below stay inside these ranges and needn't reach their ends.
Inputs may be any that keep to these rules, and one draw needn't show every extreme that they name: Slot j of device (t, p) holds a scan position exactly when j < live_count[t, p]; some device holds 32.
All inputs are finite; a program needn't handle non-finite values.
Results may differ from the reference program's by a relative error of at most 0.0003.
Values sent between devices are 32-bit elements; how exact they have to be, the bound alone decides.
A program may use at most 64 MiB of HBM per device.

```python
import jax
import jax.numpy as jnp
from jax import lax

PATCH = 128
STRIP = 128
COLS = 1024
POS_CAP = 32
ITERS = 2
ROWS = 2048
SLOTS = 1024
N_TILE = 16
N_POS = 2


def draw_object_field(key, part):
    row_place = jnp.arange(ROWS, dtype=jnp.float32)
    row_scale = 0.45 * jnp.exp(jnp.log(3.0) * row_place / ROWS)
    key_base, key_rough = jax.random.split(key)
    base_values = jnp.clip(jax.random.normal(key_base, (2, ROWS, COLS), jnp.float32), -5.0, 5.0)
    rough_factor = jnp.exp(jax.random.uniform(key_rough, (2, ROWS, COLS), jnp.float32, -0.35, 0.35))
    return base_values * rough_factor * row_scale[None, :, None]


def draw_live_count(key, part):
    lowest = max(1, POS_CAP // 4)
    spread = max(POS_CAP - lowest, 1)
    raw_draw = jax.random.randint(key, (N_TILE, N_POS), 0, POS_CAP - lowest + 1, dtype=jnp.int32)
    counts = lowest + raw_draw * raw_draw // spread
    counts = jnp.minimum(counts, POS_CAP)
    counts = counts.at[0, 0].set(POS_CAP)
    counts = counts.at[N_TILE - 1, N_POS - 1].set(lowest)
    return counts.astype(jnp.int32)


def touch_ends(result, key, low, top_value):
    longest = result.shape.index(max(result.shape))
    spots = []
    for shift in (0, 1):
        where = [jax.random.randint(jax.random.fold_in(key, axis), (), 0, length) for axis, length in enumerate(result.shape)]
        where[longest] = (where[longest] + shift) % result.shape[longest]
        spots.append(tuple(where))
    return result.at[spots[0]].set(low).at[spots[1]].set(top_value)


def level_of(stream_key, shape, cuts, least, largest):
    loudness, own = 1.0, jax.random.fold_in(stream_key, 6)
    for position, blocks in cuts:
        steps = jnp.exp(jax.random.uniform(jax.random.fold_in(own, position), (blocks,), jnp.float32, least / len(cuts), largest / len(cuts)))
        loudness = loudness * jnp.repeat(steps, shape[position] // blocks).reshape([-1 if axis == position else 1 for axis in range(len(shape))])
    return loudness


def noise(stream_key, extent, scale, bound, held_as=jnp.bfloat16):
    array = jax.random.normal(stream_key, extent, jnp.float32) * scale
    return jnp.minimum(jnp.maximum(array, -bound), bound).astype(held_as)


def setup_inputs(seed: int = 0) -> dict:
    key_of = jax.random.split(jax.random.key(seed), 7)
    return {
        "object_field": draw_object_field(jax.random.fold_in(key_of[6], 71), 0),
        "probe_field": noise(key_of[1], (2, PATCH, PATCH), 0.7, 4.0, jnp.float32),
        "amplitudes": jnp.clip(2.0 * jax.random.uniform(key_of[2], (N_TILE, N_POS, POS_CAP, PATCH, PATCH), jnp.float32) ** level_of(key_of[2], (N_TILE, N_POS, POS_CAP, PATCH, PATCH), ((0, 16), (1, 2)), -0.2, 0.2), 0.0, 2.0),
        "scan_rows": touch_ends(jax.random.randint(key_of[3], (N_TILE, N_POS, POS_CAP), 0, STRIP), jax.random.fold_in(key_of[3], 1), 0, STRIP - 1).astype(jnp.int32),
        "scan_cols": touch_ends(jax.random.randint(key_of[4], (N_TILE, N_POS, POS_CAP), 0, COLS), jax.random.fold_in(key_of[4], 1), 0, COLS - 1).astype(jnp.int32),
        "live_count": draw_live_count(jax.random.fold_in(key_of[6], 71), 0),
    }


MODULUS_FLOOR = 0.2
OBJECT_RELAX = 1.0

def tile_update(extended, probe_field, tile_amps, tile_rows, tile_cols, tile_counts, tile_number):
    zero_index = jnp.zeros((), jnp.int32)
    band_row = (tile_number * STRIP).astype(jnp.int32)
    strip_band = lax.dynamic_slice(extended, (zero_index, band_row, zero_index), (2, 2 * STRIP, COLS + PATCH))
    slot_number = jnp.arange(POS_CAP, dtype=jnp.int32)
    live_mask = (slot_number[None, :] < tile_counts[:, None]).reshape(-1)
    probe_real = probe_field[0]
    probe_imag = probe_field[1]

    def visit_position(state_pair, item_tuple):
        band_sums, probe_sums = state_pair
        amplitude, row_start, col_start, is_live = item_tuple
        corner = (zero_index, row_start.astype(jnp.int32), col_start.astype(jnp.int32))
        patch_wave = lax.dynamic_slice(strip_band, corner, (2, PATCH, PATCH))
        exit_wave = probe_real * patch_wave[0] - probe_imag * patch_wave[1] + 1j * (probe_real * patch_wave[1] + probe_imag * patch_wave[0])
        far_field = jnp.fft.fft2(exit_wave, norm='ortho')
        magnitude = jnp.sqrt(far_field.real ** 2 + far_field.imag ** 2)
        projected = far_field * (amplitude / jnp.maximum(magnitude, MODULUS_FLOOR))
        revised = jnp.fft.ifft2(projected, norm='ortho')
        back_real = revised.real
        back_imag = revised.imag
        object_terms = jnp.stack([probe_real * back_real + probe_imag * back_imag, probe_real * back_imag - probe_imag * back_real, probe_real * probe_real + probe_imag * probe_imag])
        object_terms = jnp.where(is_live, object_terms, 0.0)
        probe_terms = jnp.stack([patch_wave[0] * back_real + patch_wave[1] * back_imag, patch_wave[0] * back_imag - patch_wave[1] * back_real, patch_wave[0] * patch_wave[0] + patch_wave[1] * patch_wave[1]])
        probe_terms = jnp.where(is_live, probe_terms, 0.0)
        current = lax.dynamic_slice(band_sums, corner, (3, PATCH, PATCH))
        band_sums = lax.dynamic_update_slice(band_sums, current + object_terms, corner)
        return ((band_sums, probe_sums + probe_terms), None)
    initial = (jnp.zeros((3, 2 * STRIP, COLS + PATCH), jnp.float32), jnp.zeros((3, PATCH, PATCH), jnp.float32))
    items = (tile_amps.reshape(-1, PATCH, PATCH), tile_rows.reshape(-1), tile_cols.reshape(-1), live_mask)
    finals, unused = lax.scan(visit_position, initial, items)
    return finals

def one_round(object_field, probe_field, amplitudes, scan_rows, scan_cols, live_count):
    extended = jnp.concatenate([object_field, object_field[:, :STRIP]], axis=1)
    extended = jnp.concatenate([extended, extended[:, :, :PATCH]], axis=2)
    tile_numbers = jnp.arange(N_TILE, dtype=jnp.int32)

    def per_tile(item_tuple):
        tile_number, tile_amps, tile_rows, tile_cols, tile_counts = item_tuple
        return tile_update(extended, probe_field, tile_amps, tile_rows, tile_cols, tile_counts, tile_number)
    band_sums, probe_sums = lax.map(per_tile, (tile_numbers, amplitudes, scan_rows, scan_cols, live_count))
    folded = band_sums[..., :COLS].at[..., :PATCH].add(band_sums[..., COLS:])
    strip_sums = folded[:, :, :STRIP] + jnp.roll(folded[:, :, STRIP:], 1, axis=0)
    object_sums = jnp.transpose(strip_sums, (1, 0, 2, 3)).reshape(3, ROWS, COLS)
    object_next = (object_sums[:2] + OBJECT_RELAX * object_field) / (object_sums[2] + OBJECT_RELAX)[None]
    probe_total = lax.optimization_barrier(jnp.sum(probe_sums, axis=0))
    probe_relax = SLOTS / 4.0
    probe_next = (probe_total[:2] + probe_relax * probe_field) / (probe_total[2] + probe_relax)[None]
    return (object_next, probe_next)

def reference(object_field, probe_field, amplitudes, scan_rows, scan_cols, live_count):
    for round_number in range(ITERS):
        object_field, probe_field = one_round(object_field, probe_field, amplitudes, scan_rows, scan_cols, live_count)
    return (object_field, probe_field)
```

```python
import math

import jax
import jax.numpy as jnp
import ml_dtypes
import numpy as np
from jax import lax
from jax.experimental import pallas as pl
from jax.experimental.pallas import tpu as pltpu
from jax.sharding import PartitionSpec as P

ITERS = 2
MODULUS_FLOOR = 0.2
OBJECT_RELAX = 1.0
LANES = 128
F32 = jnp.float32
BF16 = jnp.bfloat16


def shift_pos(value):
    n = lax.axis_size("pos")
    return lax.ppermute(value, "pos", [(i, i ^ 1) for i in range(n)])


def shift_tile(value, step):
    n = lax.axis_size("tile")
    return lax.ppermute(value, "tile", [(i, (i + step) % n) for i in range(n)])


def shift_both(value, step):
    n, m = lax.axis_size("tile"), lax.axis_size("pos")
    route = [
        (t * m + p, ((t + step) % n) * m + (p ^ 1)) for t in range(n) for p in range(m)
    ]
    return lax.ppermute(value, ("tile", "pos"), route)


def split_table(table):
    high = table.astype(ml_dtypes.bfloat16)
    low = (table - high.astype(np.float64)).astype(ml_dtypes.bfloat16)
    return high, low


def dft_tables(size):
    k = np.arange(size)
    angle = (k[:, None] * k[None, :] % size) * (2.0 * math.pi / size)
    c = np.cos(angle) / math.sqrt(size)
    s = np.sin(angle) / math.sqrt(size)
    first = np.block([[c, -s], [s, c]])
    second = np.block([[c, s], [-s, c]])
    return np.stack([*split_table(first), *split_table(second)])


def split(value):
    high = value.astype(BF16)
    low = (value - high.astype(F32)).astype(BF16)
    return high, low


def dot(a, b):
    return jnp.dot(a, b, preferred_element_type=F32)


def right_product(value, table_h, table_l):
    high, low = split(value)
    return dot(high, table_h) + (dot(low, table_h) + dot(high, table_l))


def left_product(table_h, table_l, value):
    high, low = split(value)
    return dot(table_h, high) + (dot(table_h, low) + dot(table_l, high))


def visit_kernel(
    meta, slots, rows, cols, probe, amps, own_a, own_b, next_a, next_b, tables,
    sums_a, sums_b, probe_sums, band, acc,
):
    patch = probe.shape[1]
    half_tiles = own_a.shape[2] // LANES
    tiles = 2 * half_tiles
    strip = own_a.shape[1]
    total = meta[0]
    base_a = meta[1] * half_tiles
    base_b = half_tiles - base_a
    for plane in range(2):
        for k in range(half_tiles):
            lanes = slice(k * LANES, (k + 1) * LANES)
            band[plane, base_a + k, :strip, :] = own_a[plane, :, lanes]
            band[plane, base_b + k, :strip, :] = own_b[plane, :, lanes]
            band[plane, base_a + k, strip:, :] = next_a[plane, :, lanes]
            band[plane, base_b + k, strip:, :] = next_b[plane, :, lanes]
    acc[...] = jnp.zeros_like(acc)
    probe_sums[...] = jnp.zeros_like(probe_sums)
    lane = lax.broadcasted_iota(jnp.int32, (patch, LANES), 1)

    def place(j):
        col = cols[j]
        q = col // LANES
        return rows[j], q, lax.rem(q + 1, tiles), lax.rem(col, LANES)

    def cut(j):
        r, q, q2, s = place(j)
        back = lax.rem(LANES - s, LANES)
        parts = []
        for plane in range(2):
            left = band[plane, q, pl.ds(r, patch), :]
            right = band[plane, q2, pl.ds(r, patch), :]
            parts.append(pltpu.roll(jnp.where(lane >= s, left, right), back, 1))
        return parts

    def body(step, carry):
        pr, pi = probe[0], probe[1]
        js = [2 * step, 2 * step + 1]
        live = [jnp.where(j < total, 1.0, 0.0).astype(F32) for j in js]
        patches = [cut(j) for j in js]
        exits = [
            jnp.concatenate([pr * a - pi * b, pr * b + pi * a], axis=1) for a, b in patches
        ]
        z = right_product(jnp.concatenate(exits, axis=0), tables[0], tables[1])
        z = jnp.concatenate(
            [
                jnp.concatenate([z[m * patch : (m + 1) * patch, c * LANES : (c + 1) * LANES] for c in range(2)], axis=0)
                for m in range(2)
            ],
            axis=1,
        )
        far = left_product(tables[2], tables[3], z)
        fr, fi = far[:patch], far[patch:]
        power = jnp.maximum(fr * fr + fi * fi, MODULUS_FLOOR * MODULUS_FLOOR)
        amp = jnp.concatenate([amps[slots[j]] * f for j, f in zip(js, live)], axis=1)
        ratio = amp * lax.rsqrt(power)
        projected = jnp.concatenate([fr * ratio, fi * ratio], axis=0)
        y = left_product(tables[0], tables[1], projected)
        y = jnp.concatenate(
            [
                jnp.concatenate([y[c * patch : (c + 1) * patch, m * LANES : (m + 1) * LANES] for c in range(2)], axis=1)
                for m in range(2)
            ],
            axis=0,
        )
        back = right_product(y, tables[2], tables[3])
        backs = [
            (back[m * patch : (m + 1) * patch, :LANES], back[m * patch : (m + 1) * patch, LANES:])
            for m in range(2)
        ]
        (ar, ai), (br, bi) = patches
        (ur, ui), (vr, vi) = backs
        probe_sums[0] += (ar * ur + ai * ui) + (br * vr + bi * vi)
        probe_sums[1] += (ar * ui - ai * ur) + (br * vi - bi * vr)
        probe_sums[2] += live[0] * (ar * ar + ai * ai) + live[1] * (br * br + bi * bi)
        for j, (er, ei) in zip(js, backs):
            r, q, q2, s = place(j)
            ahead = lane >= s
            for plane, term in enumerate((pr * er + pi * ei, pr * ei - pi * er)):
                turned = pltpu.roll(term, s, 1)
                acc[plane, q, pl.ds(r, patch), :] += jnp.where(ahead, turned, 0.0)
                acc[plane, q2, pl.ds(r, patch), :] += jnp.where(ahead, 0.0, turned)
        return carry

    lax.fori_loop(0, (total + 1) // 2, body, 0)
    for plane in range(2):
        for k in range(half_tiles):
            lanes = slice(k * LANES, (k + 1) * LANES)
            sums_a[plane, :, lanes] = acc[plane, base_a + k]
            sums_b[plane, :, lanes] = acc[plane, base_b + k]


def visit(meta, slots, rows, cols, probe, amps, own_a, own_b, next_a, next_b, tables):
    planes, strip, half = own_a.shape
    tiles = 2 * half // LANES
    smem = pl.BlockSpec(memory_space=pltpu.SMEM)
    vmem = pl.BlockSpec(memory_space=pltpu.VMEM)
    return pl.pallas_call(
        visit_kernel,
        out_shape=(
            jax.ShapeDtypeStruct((2, 2 * strip, half), F32),
            jax.ShapeDtypeStruct((2, 2 * strip, half), F32),
            jax.ShapeDtypeStruct((3,) + probe.shape[1:], F32),
        ),
        in_specs=[smem] * 4 + [vmem] * 7,
        out_specs=(vmem, vmem, vmem),
        scratch_shapes=[
            pltpu.VMEM((2, tiles, 2 * strip, LANES), F32),
            pltpu.VMEM((2, tiles, 2 * strip, LANES), F32),
        ],
        name="visit",
        cost_estimate=pl.CostEstimate(flops=10**10, bytes_accessed=10**7, transcendentals=0),
    )(meta, slots, rows, cols, probe, amps, own_a, own_b, next_a, next_b, tables)


def weight_kernel(meta, counts, rows, cols, probe, out, acc):
    patch = probe.shape[1]
    strip = out.shape[0]
    half_tiles = out.shape[1] // LANES
    tiles = 2 * half_tiles
    base = meta[1] * half_tiles
    acc[...] = jnp.zeros_like(acc)
    lane = lax.broadcasted_iota(jnp.int32, (patch, LANES), 1)

    for group in range(4):
        down = strip if group < 2 else 0

        def body(j, carry):
            pr, pi = probe[0], probe[1]
            power = pr * pr + pi * pi
            col = cols[group, j]
            r = rows[group, j] + down
            q, s = col // LANES, lax.rem(col, LANES)
            q1 = q - base
            q2 = lax.rem(q + 1, tiles) - base
            ahead = lane >= s
            in1 = jnp.logical_and(q1 >= 0, q1 < half_tiles)
            in2 = jnp.logical_and(q2 >= 0, q2 < half_tiles)

            @pl.when(in1)
            def _():
                acc[q1, pl.ds(r, patch), :] += jnp.where(ahead, pltpu.roll(power, s, 1), 0.0)

            @pl.when(in2)
            def _():
                acc[q2, pl.ds(r, patch), :] += jnp.where(ahead, 0.0, pltpu.roll(power, s, 1))

            return carry

        lax.fori_loop(0, counts[group], body, 0)
    for k in range(half_tiles):
        out[:, k * LANES : (k + 1) * LANES] = acc[k, strip : 2 * strip, :] + OBJECT_RELAX


def weights(meta, counts, rows, cols, probe, strip, half):
    smem = pl.BlockSpec(memory_space=pltpu.SMEM)
    vmem = pl.BlockSpec(memory_space=pltpu.VMEM)
    return pl.pallas_call(
        weight_kernel,
        out_shape=jax.ShapeDtypeStruct((strip, half), F32),
        in_specs=[smem] * 4 + [vmem],
        out_specs=vmem,
        scratch_shapes=[pltpu.VMEM((half // LANES, 3 * strip, LANES), F32)],
        name="weights",
        cost_estimate=pl.CostEstimate(flops=10**9, bytes_accessed=10**6, transcendentals=0),
    )(meta, counts, rows, cols, probe)


def on_device(object_field, probe_field, amplitudes, scan_rows, scan_cols, live_count):
    core = lax.axis_index("pos")
    own_amps = amplitudes[0, 0]
    slot_count = own_amps.shape[0]
    window = 3 * slot_count // 8
    strip, columns = object_field.shape[1:]
    half = columns // 2
    patch = probe_field.shape[1]
    tables = jnp.asarray(dft_tables(patch))

    own_total = live_count[0, 0]
    own_first = jnp.maximum(own_total - window, 0)
    sent_amps = lax.dynamic_slice(own_amps, (own_first, 0, 0), (window, patch, patch))
    own_list = jnp.concatenate([scan_rows[0, 0], scan_cols[0, 0], live_count[0]])
    mate_list = shift_pos(own_list)
    mate_amps = shift_pos(sent_amps)
    above_list = shift_tile(own_list, 1)
    above_mate = shift_both(own_list, 1)
    lists = jnp.stack([own_list, mate_list, above_list, above_mate])
    all_rows, all_cols = lists[:, :slot_count], lists[:, slot_count : 2 * slot_count]
    counts = lists[:, 2 * slot_count]

    mate_total = counts[1]
    given = jnp.maximum(own_total - mate_total, 0) // 2
    taken = jnp.maximum(mate_total - own_total, 0) // 2
    kept = own_total - given
    here = kept + taken
    place = jnp.arange(slot_count + 2, dtype=jnp.int32)
    taken_index = mate_total - taken + (place - kept)
    mine = place < kept
    taken_slot = slot_count + taken_index - jnp.maximum(mate_total - window, 0)
    slots = jnp.clip(jnp.where(mine, place, taken_slot), 0, slot_count + window - 1)
    safe_own = jnp.clip(place, 0, slot_count - 1)
    safe_mate = jnp.clip(taken_index, 0, slot_count - 1)
    rows = jnp.where(mine, scan_rows[0, 0][safe_own], all_rows[1][safe_mate])
    cols = jnp.where(mine, scan_cols[0, 0][safe_own], all_cols[1][safe_mate])
    meta = jnp.stack([here, core.astype(jnp.int32)])
    amps = jnp.concatenate([own_amps, mate_amps])

    probe_relax = slot_count * lax.axis_size("tile") * lax.axis_size("pos") / 4.0
    own_a = lax.dynamic_slice(object_field, (0, 0, core * half), (2, strip, half))
    own_b = lax.dynamic_slice(object_field, (0, 0, (1 - core) * half), (2, strip, half))
    for round_number in range(ITERS):
        next_a = shift_tile(own_a, -1)
        next_b = shift_pos(next_a)
        weight = weights(meta, counts, all_rows, all_cols, probe_field, strip, half)
        sums_a, sums_b, probe_sums = visit(
            meta, slots, rows, cols, probe_field, amps, own_a, own_b, next_a, next_b, tables
        )
        mate_sums = shift_pos(sums_b)
        spill = sums_a[:, strip:] + mate_sums[:, strip:]
        from_above = shift_tile(spill, 1)
        probe_total = lax.psum(probe_sums, ("tile", "pos"))
        own_sums = sums_a[:, :strip] + mate_sums[:, :strip] + from_above
        own_a = (own_sums + OBJECT_RELAX * own_a) / weight[None]
        own_b = shift_pos(own_a)
        probe_field = (probe_total[:2] + probe_relax * probe_field) / (
            probe_total[2] + probe_relax
        )[None]
    left = jnp.where(core == 0, own_a, own_b)
    right = jnp.where(core == 0, own_b, own_a)
    return (jnp.concatenate([left, right], axis=2), probe_field)


def solution(mesh):
    placed = (
        P(None, "tile", None),
        P(),
        P("tile", "pos", None, None, None),
        P("tile", "pos", None),
        P("tile", "pos", None),
        P("tile", "pos"),
    )
    return jax.shard_map(
        on_device,
        mesh=mesh,
        in_specs=placed,
        out_specs=(P(None, "tile", None), P()),
        check_vma=False,
    )
```

```python
import math

import jax
import jax.numpy as jnp
import ml_dtypes
import numpy as np
from jax import lax
from jax.experimental import pallas as pl
from jax.experimental.pallas import tpu as pltpu
from jax.sharding import PartitionSpec as P

ITERS = 2
MODULUS_FLOOR = 0.2
OBJECT_RELAX = 1.0
LANES = 128
F32 = jnp.float32
BF16 = jnp.bfloat16


def shift_pos(value):
    n = lax.axis_size("pos")
    return lax.ppermute(value, "pos", [(i, i ^ 1) for i in range(n)])


def shift_tile(value, step):
    n = lax.axis_size("tile")
    return lax.ppermute(value, "tile", [(i, (i + step) % n) for i in range(n)])


def shift_both(value, step):
    n, m = lax.axis_size("tile"), lax.axis_size("pos")
    route = [
        (t * m + p, ((t + step) % n) * m + (p ^ 1)) for t in range(n) for p in range(m)
    ]
    return lax.ppermute(value, ("tile", "pos"), route)


def split_table(table):
    high = table.astype(ml_dtypes.bfloat16)
    low = (table - high.astype(np.float64)).astype(ml_dtypes.bfloat16)
    return high, low


def dft_tables(size):
    k = np.arange(size)
    angle = (k[:, None] * k[None, :] % size) * (2.0 * math.pi / size)
    c = np.cos(angle) / math.sqrt(size)
    s = np.sin(angle) / math.sqrt(size)
    first = np.block([[c, -s], [s, c]])
    second = np.block([[c, s], [-s, c]])
    return np.stack([*split_table(first), *split_table(second)])


def split(value):
    high = value.astype(BF16)
    low = (value - high.astype(F32)).astype(BF16)
    return high, low


def dot(a, b):
    return jnp.dot(a, b, preferred_element_type=F32)


def right_product(value, table_h, table_l):
    high, low = split(value)
    return dot(high, table_h) + (dot(low, table_h) + dot(high, table_l))


def left_product(table_h, table_l, value):
    high, low = split(value)
    return dot(table_h, high) + (dot(table_h, low) + dot(table_l, high))


def visit_kernel(
    meta, slots, rows, cols, probe, amps, own_a, own_b, next_a, next_b, tables,
    sums_a, sums_b, probe_sums, band, acc,
):
    patch = probe.shape[1]
    half_tiles = own_a.shape[2] // LANES
    tiles = 2 * half_tiles
    strip = own_a.shape[1]
    total = meta[0]
    base_a = meta[1] * half_tiles
    base_b = half_tiles - base_a
    for plane in range(2):
        for k in range(half_tiles):
            lanes = slice(k * LANES, (k + 1) * LANES)
            band[plane, base_a + k, :strip, :] = own_a[plane, :, lanes]
            band[plane, base_b + k, :strip, :] = own_b[plane, :, lanes]
            band[plane, base_a + k, strip:, :] = next_a[plane, :, lanes]
            band[plane, base_b + k, strip:, :] = next_b[plane, :, lanes]
    acc[...] = jnp.zeros_like(acc)
    probe_sums[...] = jnp.zeros_like(probe_sums)
    lane = lax.broadcasted_iota(jnp.int32, (patch, LANES), 1)

    def place(j):
        col = cols[j]
        q = col // LANES
        return rows[j], q, lax.rem(q + 1, tiles), lax.rem(col, LANES)

    def cut(j):
        r, q, q2, s = place(j)
        back = lax.rem(LANES - s, LANES)
        parts = []
        for plane in range(2):
            left = band[plane, q, pl.ds(r, patch), :]
            right = band[plane, q2, pl.ds(r, patch), :]
            parts.append(pltpu.roll(jnp.where(lane >= s, left, right), back, 1))
        return parts

    def body(step, carry):
        pr, pi = probe[0], probe[1]
        js = [2 * step, 2 * step + 1]
        live = [jnp.where(j < total, 1.0, 0.0).astype(F32) for j in js]
        patches = [cut(j) for j in js]
        exits = [
            jnp.concatenate([pr * a - pi * b, pr * b + pi * a], axis=1) for a, b in patches
        ]
        z = right_product(jnp.concatenate(exits, axis=0), tables[0], tables[1])
        z = jnp.concatenate(
            [
                jnp.concatenate([z[m * patch : (m + 1) * patch, c * LANES : (c + 1) * LANES] for c in range(2)], axis=0)
                for m in range(2)
            ],
            axis=1,
        )
        far = left_product(tables[2], tables[3], z)
        fr, fi = far[:patch], far[patch:]
        power = jnp.maximum(fr * fr + fi * fi, MODULUS_FLOOR * MODULUS_FLOOR)
        amp = jnp.concatenate([amps[slots[j]] * f for j, f in zip(js, live)], axis=1)
        ratio = amp * lax.rsqrt(power)
        projected = jnp.concatenate([fr * ratio, fi * ratio], axis=0)
        y = left_product(tables[0], tables[1], projected)
        y = jnp.concatenate(
            [
                jnp.concatenate([y[c * patch : (c + 1) * patch, m * LANES : (m + 1) * LANES] for c in range(2)], axis=1)
                for m in range(2)
            ],
            axis=0,
        )
        back = right_product(y, tables[2], tables[3])
        backs = [
            (back[m * patch : (m + 1) * patch, :LANES], back[m * patch : (m + 1) * patch, LANES:])
            for m in range(2)
        ]
        (ar, ai), (br, bi) = patches
        (ur, ui), (vr, vi) = backs
        probe_sums[0] += (ar * ur + ai * ui) + (br * vr + bi * vi)
        probe_sums[1] += (ar * ui - ai * ur) + (br * vi - bi * vr)
        probe_sums[2] += live[0] * (ar * ar + ai * ai) + live[1] * (br * br + bi * bi)
        for j, (er, ei) in zip(js, backs):
            r, q, q2, s = place(j)
            ahead = lane >= s
            for plane, term in enumerate((pr * er + pi * ei, pr * ei - pi * er)):
                turned = pltpu.roll(term, s, 1)
                acc[plane, q, pl.ds(r, patch), :] += jnp.where(ahead, turned, 0.0)
                acc[plane, q2, pl.ds(r, patch), :] += jnp.where(ahead, 0.0, turned)
        return carry

    lax.fori_loop(0, (total + 1) // 2, body, 0)
    for plane in range(2):
        for k in range(half_tiles):
            lanes = slice(k * LANES, (k + 1) * LANES)
            sums_a[plane, :, lanes] = acc[plane, base_a + k]
            sums_b[plane, :, lanes] = acc[plane, base_b + k]


def visit(meta, slots, rows, cols, probe, amps, own_a, own_b, next_a, next_b, tables):
    planes, strip, half = own_a.shape
    tiles = 2 * half // LANES
    smem = pl.BlockSpec(memory_space=pltpu.SMEM)
    vmem = pl.BlockSpec(memory_space=pltpu.VMEM)
    return pl.pallas_call(
        visit_kernel,
        out_shape=(
            jax.ShapeDtypeStruct((2, 2 * strip, half), F32),
            jax.ShapeDtypeStruct((2, 2 * strip, half), F32),
            jax.ShapeDtypeStruct((3,) + probe.shape[1:], F32),
        ),
        in_specs=[smem] * 4 + [vmem] * 7,
        out_specs=(vmem, vmem, vmem),
        scratch_shapes=[
            pltpu.VMEM((2, tiles, 2 * strip, LANES), F32),
            pltpu.VMEM((2, tiles, 2 * strip, LANES), F32),
        ],
        name="visit",
        cost_estimate=pl.CostEstimate(flops=10**10, bytes_accessed=10**7, transcendentals=0),
    )(meta, slots, rows, cols, probe, amps, own_a, own_b, next_a, next_b, tables)


def weight_kernel(meta, counts, rows, cols, probe, out, acc, power):
    patch = probe.shape[1]
    strip = out.shape[0]
    half_tiles = out.shape[1] // LANES
    tiles = 2 * half_tiles
    last = rows.shape[1] - 1
    base = meta[1] * half_tiles
    acc[...] = jnp.zeros_like(acc)
    power[...] = probe[0] * probe[0] + probe[1] * probe[1]
    lane = lax.broadcasted_iota(jnp.int32, (patch, LANES), 1)

    for group in range(4):
        down = strip if group < 2 else 0

        def body(step, carry):
            for member in range(2):
                j = 2 * step + member
                live = j < counts[group]
                j = jnp.minimum(j, last)
                col = cols[group, j]
                r = rows[group, j] + down
                q, s = col // LANES, lax.rem(col, LANES)
                q1 = q - base
                q2 = lax.rem(q + 1, tiles) - base
                in1 = jnp.logical_and(live, jnp.logical_and(q1 >= 0, q1 < half_tiles))
                in2 = jnp.logical_and(live, jnp.logical_and(q2 >= 0, q2 < half_tiles))
                q1 = jnp.where(in1, q1, half_tiles)
                q2 = jnp.where(in2, q2, half_tiles + 1)
                turned = pltpu.roll(power[...], s, 1)
                ahead = lane >= s
                acc[q1, pl.ds(r, patch), :] += jnp.where(ahead, turned, 0.0)
                acc[q2, pl.ds(r, patch), :] += jnp.where(ahead, 0.0, turned)
            return carry

        lax.fori_loop(0, (counts[group] + 1) // 2, body, 0)
    for k in range(half_tiles):
        out[:, k * LANES : (k + 1) * LANES] = acc[k, strip : 2 * strip, :] + OBJECT_RELAX


def weights(meta, counts, rows, cols, probe, strip, half):
    smem = pl.BlockSpec(memory_space=pltpu.SMEM)
    vmem = pl.BlockSpec(memory_space=pltpu.VMEM)
    return pl.pallas_call(
        weight_kernel,
        out_shape=jax.ShapeDtypeStruct((strip, half), F32),
        in_specs=[smem] * 4 + [vmem],
        out_specs=vmem,
        scratch_shapes=[
            pltpu.VMEM((half // LANES + 2, 3 * strip, LANES), F32),
            pltpu.VMEM(probe.shape[1:], F32),
        ],
        name="weights",
        cost_estimate=pl.CostEstimate(flops=10**9, bytes_accessed=10**6, transcendentals=0),
    )(meta, counts, rows, cols, probe)


def exchange_kernel(
    final, n_tile, relax, sums_a, sums_b, own, weight, probe_sums, probe, *refs
):
    if final:
        own_a, own_b, probe_next = refs[:3]
        refs = refs[3:]
    else:
        own_a, own_b, next_a, next_b, probe_next = refs[:5]
        refs = refs[5:]
    land_o, spill, land_s, fresh, land_b, land_na, land_nb, p_out, p_land, p_new, p_got, send, recv = refs
    strip = own.shape[1]
    rows = p_new.shape[1]
    tile, core = lax.axis_index("tile"), lax.axis_index("pos")
    mate = (tile, 1 - core)
    below = (lax.rem(tile + 1, n_tile), core)
    above = (lax.rem(tile + n_tile - 1, n_tile), core)
    bits = [2**k for k in range(1, n_tile.bit_length() - 1)] + [1]
    pairs = [(tile + b - 2 * b * lax.rem(tile // b, 2), core) for b in bits]

    barrier = pltpu.get_barrier_semaphore()
    greeted = [mate, below, above] + pairs
    for other in greeted:
        pl.semaphore_signal(barrier, inc=1, device_id=other, device_id_type=pl.DeviceIdType.MESH)
    pl.semaphore_wait(barrier, len(greeted))

    used = []

    def copy(src, dst, device):
        k = len(used)
        made = pltpu.make_async_remote_copy(
            src_ref=src, dst_ref=dst, send_sem=send.at[k], recv_sem=recv.at[k],
            device_id=device, device_id_type=pl.DeviceIdType.MESH,
        )
        used.append(made)
        made.start()
        return made

    down = slice(strip, 2 * strip)
    mine = pl.ds(pl.multiple_of(core * rows, rows), rows)
    theirs = pl.ds(pl.multiple_of((1 - core) * rows, rows), rows)
    got_s = [copy(sums_b.at[k, down], land_o.at[k, down], mate) for k in range(2)]
    got_p = copy(probe_sums.at[:, theirs], p_land.at[0], mate)
    got_o = [copy(sums_b.at[k, :strip], land_o.at[k, :strip], mate) for k in range(2)]
    got_spill = []
    for k in range(2):
        got_s[k].wait_recv()
        spill[k] = sums_a[k, down] + land_o[k, down]
        got_spill.append(copy(spill.at[k], land_s.at[k], below))
    got_p.wait_recv()
    p_out[0] = probe_sums[:, mine] + p_land[0]
    for stage in range(len(bits) - 1):
        got_p = copy(p_out.at[stage], p_land.at[stage + 1], pairs[stage])
        if stage < 2:
            got_o[stage].wait_recv()
            fresh[stage] = sums_a[stage, :strip] + land_o[stage, :strip] + OBJECT_RELAX * own[stage]
        got_p.wait_recv()
        p_out[stage + 1] = p_out[stage] + p_land[stage + 1]
    stage = len(bits) - 1
    got_p = copy(p_out.at[stage], p_land.at[stage + 1], pairs[stage])
    got_b, got_next = [], []
    for k in range(2):
        got_spill[k].wait_recv()
        own_a[k] = (fresh[k] + land_s[k]) / weight[...]
        if not final:
            got_next.append(copy(own_a.at[k], land_na.at[k], above))
        got_b.append(copy(own_a.at[k], land_b.at[k], mate))
    got_p.wait_recv()
    total = p_out[stage] + p_land[stage + 1]
    old = probe[:, mine]
    p_new[...] = (total[:2] + relax * old) / (total[2] + relax)[None]
    got_p = copy(p_new, p_got, mate)
    probe_next[:, mine] = p_new[...]
    got_p.wait_recv()
    probe_next[:, theirs] = p_got[...]
    for k in range(2):
        got_b[k].wait_recv()
        own_b[k] = land_b[k]
    if not final:
        got_last = []
        for k in range(2):
            got_next[k].wait_recv()
            got_last.append(copy(land_na.at[k], land_nb.at[k], mate))
            next_a[k] = land_na[k]
        for k in range(2):
            got_last[k].wait_recv()
            next_b[k] = land_nb[k]
    for made in used:
        made.wait_send()


def exchange(final, relax, sums_a, sums_b, own, weight, probe_sums, probe):
    n_tile = lax.axis_size("tile")
    vmem = pl.BlockSpec(memory_space=pltpu.VMEM)
    strip_like = jax.ShapeDtypeStruct(own.shape, F32)
    outs = [strip_like] * (2 if final else 4) + [jax.ShapeDtypeStruct(probe.shape, F32)]
    stages = n_tile.bit_length() - 1
    rows = probe.shape[1] // 2
    width = probe.shape[2]
    block = pltpu.VMEM(own.shape, F32)
    return pl.pallas_call(
        lambda *refs: exchange_kernel(final, n_tile, relax, *refs),
        out_shape=outs,
        in_specs=[vmem] * 6,
        out_specs=[vmem] * len(outs),
        scratch_shapes=[
            pltpu.VMEM(sums_a.shape, F32),
            block, block, block, block, block, block,
            pltpu.VMEM((stages, 3, rows, width), F32),
            pltpu.VMEM((stages + 1, 3, rows, width), F32),
            pltpu.VMEM((2, rows, width), F32),
            pltpu.VMEM((2, rows, width), F32),
            pltpu.SemaphoreType.DMA((stages + 14,)),
            pltpu.SemaphoreType.DMA((stages + 14,)),
        ],
        compiler_params=pltpu.CompilerParams(
            collective_id=1 if final else 0, has_side_effects=True
        ),
        name="exchange",
    )(sums_a, sums_b, own, weight, probe_sums, probe)


def on_device(object_field, probe_field, amplitudes, scan_rows, scan_cols, live_count):
    core = lax.axis_index("pos")
    own_amps = amplitudes[0, 0]
    slot_count = own_amps.shape[0]
    window = 3 * slot_count // 8
    strip, columns = object_field.shape[1:]
    half = columns // 2
    patch = probe_field.shape[1]
    tables = jnp.asarray(dft_tables(patch))

    own_total = live_count[0, 0]
    own_first = jnp.maximum(own_total - window, 0)
    sent_amps = lax.dynamic_slice(own_amps, (own_first, 0, 0), (window, patch, patch))
    own_list = jnp.concatenate([scan_rows[0, 0], scan_cols[0, 0], live_count[0]])
    mate_list = shift_pos(own_list)
    mate_amps = shift_pos(sent_amps)
    above_list = shift_tile(own_list, 1)
    above_mate = shift_both(own_list, 1)
    lists = jnp.stack([own_list, mate_list, above_list, above_mate])
    all_rows, all_cols = lists[:, :slot_count], lists[:, slot_count : 2 * slot_count]
    counts = lists[:, 2 * slot_count]

    mate_total = counts[1]
    given = jnp.maximum(own_total - mate_total, 0) // 2
    taken = jnp.maximum(mate_total - own_total, 0) // 2
    kept = own_total - given
    here = kept + taken
    place = jnp.arange(slot_count + 2, dtype=jnp.int32)
    taken_index = mate_total - taken + (place - kept)
    mine = place < kept
    taken_slot = slot_count + taken_index - jnp.maximum(mate_total - window, 0)
    slots = jnp.clip(jnp.where(mine, place, taken_slot), 0, slot_count + window - 1)
    safe_own = jnp.clip(place, 0, slot_count - 1)
    safe_mate = jnp.clip(taken_index, 0, slot_count - 1)
    rows = jnp.where(mine, scan_rows[0, 0][safe_own], all_rows[1][safe_mate])
    cols = jnp.where(mine, scan_cols[0, 0][safe_own], all_cols[1][safe_mate])
    meta = jnp.stack([here, core.astype(jnp.int32)])
    amps = jnp.concatenate([own_amps, mate_amps])

    probe_relax = slot_count * lax.axis_size("tile") * lax.axis_size("pos") / 4.0
    own_a = lax.dynamic_slice(object_field, (0, 0, core * half), (2, strip, half))
    own_b = lax.dynamic_slice(object_field, (0, 0, (1 - core) * half), (2, strip, half))
    next_a = shift_tile(own_a, -1)
    next_b = shift_pos(next_a)
    for round_number in range(ITERS):
        weight = weights(meta, counts, all_rows, all_cols, probe_field, strip, half)
        if round_number == 0:
            meta, weight = lax.optimization_barrier((meta, weight))
        sums_a, sums_b, probe_sums = visit(
            meta, slots, rows, cols, probe_field, amps, own_a, own_b, next_a, next_b, tables
        )
        final = round_number == ITERS - 1
        results = exchange(
            final, probe_relax, sums_a, sums_b, own_a, weight, probe_sums, probe_field
        )
        if final:
            own_a, own_b, probe_field = results
        else:
            own_a, own_b, next_a, next_b, probe_field = results
    left = jnp.where(core == 0, own_a, own_b)
    right = jnp.where(core == 0, own_b, own_a)
    return (jnp.concatenate([left, right], axis=2), probe_field)


def solution(mesh):
    placed = (
        P(None, "tile", None),
        P(),
        P("tile", "pos", None, None, None),
        P("tile", "pos", None),
        P("tile", "pos", None),
        P("tile", "pos"),
    )
    return jax.shard_map(
        on_device,
        mesh=mesh,
        in_specs=placed,
        out_specs=(P(None, "tile", None), P()),
        check_vma=False,
    )
```

```python
import math

import jax
import jax.numpy as jnp
import ml_dtypes
import numpy as np
from jax import lax
from jax.experimental import pallas as pl
from jax.experimental.pallas import tpu as pltpu
from jax.sharding import PartitionSpec as P

ITERS = 2
MODULUS_FLOOR = 0.2
OBJECT_RELAX = 1.0
LANES = 128
F32 = jnp.float32
BF16 = jnp.bfloat16


def split_table(table):
    high = table.astype(ml_dtypes.bfloat16)
    low = (table - high.astype(np.float64)).astype(ml_dtypes.bfloat16)
    return high, low


def dft_tables(size):
    k = np.arange(size)
    angle = (k[:, None] * k[None, :] % size) * (2.0 * math.pi / size)
    c = np.cos(angle) / math.sqrt(size)
    s = np.sin(angle) / math.sqrt(size)
    first = np.block([[c, -s], [s, c]])
    second = np.block([[c, s], [-s, c]])
    return np.stack([*split_table(first), *split_table(second)])


def split(value):
    high = value.astype(BF16)
    low = (value - high.astype(F32)).astype(BF16)
    return high, low


def dot(a, b):
    return jnp.dot(a, b, preferred_element_type=F32)


def right_product(value, table_h, table_l):
    high, low = split(value)
    return dot(high, table_h) + (dot(low, table_h) + dot(high, table_l))


def left_product(table_h, table_l, value):
    high, low = split(value)
    return dot(table_h, high) + (dot(table_h, low) + dot(table_l, high))


def visit_kernel(
    lists, probe, amps, mate_amps, own_a, own_b, next_a, next_b, tables,
    sums_a, sums_b, probe_sums, band, acc,
):
    patch = probe.shape[1]
    half_tiles = own_a.shape[2] // LANES
    tiles = 2 * half_tiles
    strip = own_a.shape[1]
    slot_count = amps.shape[0]
    low = slot_count // 4
    own_total, mate_total = lists[0, 2, 0], lists[1, 2, 0]
    given = jnp.maximum(own_total - mate_total, 0) // 2
    kept = own_total - given
    total = kept + jnp.maximum(mate_total - own_total, 0) // 2
    base_a = lists[0, 3, 0] * half_tiles
    base_b = half_tiles - base_a
    for plane in range(2):
        for k in range(half_tiles):
            lanes = slice(k * LANES, (k + 1) * LANES)
            band[plane, base_a + k, :strip, :] = own_a[plane, :, lanes]
            band[plane, base_b + k, :strip, :] = own_b[plane, :, lanes]
            band[plane, base_a + k, strip:, :] = next_a[plane, :, lanes]
            band[plane, base_b + k, strip:, :] = next_b[plane, :, lanes]
    acc[...] = jnp.zeros_like(acc)
    probe_sums[...] = jnp.zeros_like(probe_sums)
    lane = lax.broadcasted_iota(jnp.int32, (patch, LANES), 1)

    def find(j):
        mine = j < kept
        slot = jnp.minimum(jnp.where(j < low, j, j + given), slot_count - 1)
        extra = jnp.clip(j - kept, 0, mate_amps.shape[0] - 1)
        which = jnp.where(mine, 0, 1)
        at = jnp.where(mine, slot, low + extra)
        row, col = lists[which, 0, at], lists[which, 1, at]
        q = col // LANES
        amp = jnp.where(mine, amps[slot], mate_amps[extra])
        return (row, q, lax.rem(q + 1, tiles), lax.rem(col, LANES)), amp

    def cut(place):
        r, q, q2, s = place
        back = lax.rem(LANES - s, LANES)
        parts = []
        for plane in range(2):
            left = band[plane, q, pl.ds(r, patch), :]
            right = band[plane, q2, pl.ds(r, patch), :]
            parts.append(pltpu.roll(jnp.where(lane >= s, left, right), back, 1))
        return parts

    def body(step, carry):
        pr, pi = probe[0], probe[1]
        js = [2 * step, 2 * step + 1]
        live = [jnp.where(j < total, 1.0, 0.0).astype(F32) for j in js]
        found = [find(j) for j in js]
        patches = [cut(place) for place, _ in found]
        exits = [
            jnp.concatenate([pr * a - pi * b, pr * b + pi * a], axis=1) for a, b in patches
        ]
        z = right_product(jnp.concatenate(exits, axis=0), tables[0], tables[1])
        z = jnp.concatenate(
            [
                jnp.concatenate([z[m * patch : (m + 1) * patch, c * LANES : (c + 1) * LANES] for c in range(2)], axis=0)
                for m in range(2)
            ],
            axis=1,
        )
        far = left_product(tables[2], tables[3], z)
        fr, fi = far[:patch], far[patch:]
        power = jnp.maximum(fr * fr + fi * fi, MODULUS_FLOOR * MODULUS_FLOOR)
        amp = jnp.concatenate([a * f for (_, a), f in zip(found, live)], axis=1)
        ratio = amp * lax.rsqrt(power)
        projected = jnp.concatenate([fr * ratio, fi * ratio], axis=0)
        y = left_product(tables[0], tables[1], projected)
        y = jnp.concatenate(
            [
                jnp.concatenate([y[c * patch : (c + 1) * patch, m * LANES : (m + 1) * LANES] for c in range(2)], axis=1)
                for m in range(2)
            ],
            axis=0,
        )
        back = right_product(y, tables[2], tables[3])
        backs = [
            (back[m * patch : (m + 1) * patch, :LANES], back[m * patch : (m + 1) * patch, LANES:])
            for m in range(2)
        ]
        (ar, ai), (br, bi) = patches
        (ur, ui), (vr, vi) = backs
        probe_sums[0] += (ar * ur + ai * ui) + (br * vr + bi * vi)
        probe_sums[1] += (ar * ui - ai * ur) + (br * vi - bi * vr)
        probe_sums[2] += live[0] * (ar * ar + ai * ai) + live[1] * (br * br + bi * bi)
        for ((r, q, q2, s), _), (er, ei) in zip(found, backs):
            ahead = lane >= s
            for plane, term in enumerate((pr * er + pi * ei, pr * ei - pi * er)):
                turned = pltpu.roll(term, s, 1)
                here = acc[plane, q, pl.ds(r, patch), :]
                there = acc[plane, q2, pl.ds(r, patch), :]
                acc[plane, q, pl.ds(r, patch), :] = here + jnp.where(ahead, turned, 0.0)
                acc[plane, q2, pl.ds(r, patch), :] = there + jnp.where(ahead, 0.0, turned)
        return carry

    lax.fori_loop(0, (total + 1) // 2, body, 0)
    for plane in range(2):
        for k in range(half_tiles):
            lanes = slice(k * LANES, (k + 1) * LANES)
            sums_a[plane, :, lanes] = acc[plane, base_a + k]
            sums_b[plane, :, lanes] = acc[plane, base_b + k]


def visit(lists, probe, amps, mate_amps, own_a, own_b, next_a, next_b, tables):
    planes, strip, half = own_a.shape
    tiles = 2 * half // LANES
    smem = pl.BlockSpec(memory_space=pltpu.SMEM)
    vmem = pl.BlockSpec(memory_space=pltpu.VMEM)
    return pl.pallas_call(
        visit_kernel,
        out_shape=(
            jax.ShapeDtypeStruct((2, 2 * strip, half), F32),
            jax.ShapeDtypeStruct((2, 2 * strip, half), F32),
            jax.ShapeDtypeStruct((3,) + probe.shape[1:], F32),
        ),
        in_specs=[smem] + [vmem] * 8,
        out_specs=(vmem, vmem, vmem),
        scratch_shapes=[
            pltpu.VMEM((2, tiles, 2 * strip, LANES), F32),
            pltpu.VMEM((2, tiles, 2 * strip, LANES), F32),
        ],
        name="visit",
        cost_estimate=pl.CostEstimate(flops=10**10, bytes_accessed=10**7, transcendentals=0),
    )(lists, probe, amps, mate_amps, own_a, own_b, next_a, next_b, tables)


def weight_kernel(lists, probe, out, acc, power):
    patch = probe.shape[1]
    strip = out.shape[0]
    half_tiles = out.shape[1] // LANES
    tiles = 2 * half_tiles
    last = lists.shape[2] - 1
    base = lists[0, 3, 0] * half_tiles
    acc[...] = jnp.zeros_like(acc)
    power[...] = probe[0] * probe[0] + probe[1] * probe[1]
    lane = lax.broadcasted_iota(jnp.int32, (patch, LANES), 1)

    for group in range(4):
        down = strip if group < 2 else 0

        def body(step, carry):
            for member in range(2):
                j = 2 * step + member
                live = j < lists[group, 2, 0]
                j = jnp.minimum(j, last)
                col = lists[group, 1, j]
                r = lists[group, 0, j] + down
                q, s = col // LANES, lax.rem(col, LANES)
                q1 = q - base
                q2 = lax.rem(q + 1, tiles) - base
                in1 = jnp.logical_and(live, jnp.logical_and(q1 >= 0, q1 < half_tiles))
                in2 = jnp.logical_and(live, jnp.logical_and(q2 >= 0, q2 < half_tiles))
                q1 = jnp.where(in1, q1, half_tiles)
                q2 = jnp.where(in2, q2, half_tiles + 1)
                turned = pltpu.roll(power[...], s, 1)
                ahead = lane >= s
                here = acc[q1, pl.ds(r, patch), :]
                there = acc[q2, pl.ds(r, patch), :]
                acc[q1, pl.ds(r, patch), :] = here + jnp.where(ahead, turned, 0.0)
                acc[q2, pl.ds(r, patch), :] = there + jnp.where(ahead, 0.0, turned)
            return carry

        lax.fori_loop(0, (lists[group, 2, 0] + 1) // 2, body, 0)
    for k in range(half_tiles):
        out[:, k * LANES : (k + 1) * LANES] = acc[k, strip : 2 * strip, :] + OBJECT_RELAX


def weights(lists, probe, strip, half):
    smem = pl.BlockSpec(memory_space=pltpu.SMEM)
    vmem = pl.BlockSpec(memory_space=pltpu.VMEM)
    return pl.pallas_call(
        weight_kernel,
        out_shape=jax.ShapeDtypeStruct((strip, half), F32),
        in_specs=[smem, vmem],
        out_specs=vmem,
        scratch_shapes=[
            pltpu.VMEM((half // LANES + 2, 3 * strip, LANES), F32),
            pltpu.VMEM(probe.shape[1:], F32),
        ],
        name="weights",
        cost_estimate=pl.CostEstimate(flops=10**9, bytes_accessed=10**6, transcendentals=0),
    )(lists, probe)


def exchange_kernel(
    final, n_tile, relax, sums_a, sums_b, own, weight, probe_sums, probe, *refs
):
    if final:
        own_a, own_b, probe_next = refs[:3]
        refs = refs[3:]
    else:
        own_a, own_b, next_a, next_b, probe_next = refs[:5]
        refs = refs[5:]
    land_o, spill, land_s, fresh, land_b, land_na, land_nb, p_out, p_land, p_new, p_got, send, recv = refs
    strip = own.shape[1]
    rows = p_new.shape[1]
    tile, core = lax.axis_index("tile"), lax.axis_index("pos")
    mate = (tile, 1 - core)
    below = (lax.rem(tile + 1, n_tile), core)
    above = (lax.rem(tile + n_tile - 1, n_tile), core)
    bits = [2**k for k in range(1, n_tile.bit_length() - 1)] + [1]
    pairs = [(tile + b - 2 * b * lax.rem(tile // b, 2), core) for b in bits]

    barrier = pltpu.get_barrier_semaphore()
    greeted = [mate, below, above] + pairs
    for other in greeted:
        pl.semaphore_signal(barrier, inc=1, device_id=other, device_id_type=pl.DeviceIdType.MESH)
    pl.semaphore_wait(barrier, len(greeted))

    used = []

    def copy(src, dst, device):
        k = len(used)
        made = pltpu.make_async_remote_copy(
            src_ref=src, dst_ref=dst, send_sem=send.at[k], recv_sem=recv.at[k],
            device_id=device, device_id_type=pl.DeviceIdType.MESH,
        )
        used.append(made)
        made.start()
        return made

    down = slice(strip, 2 * strip)
    mine = pl.ds(pl.multiple_of(core * rows, rows), rows)
    theirs = pl.ds(pl.multiple_of((1 - core) * rows, rows), rows)
    got_s = [copy(sums_b.at[k, down], land_o.at[k, down], mate) for k in range(2)]
    got_p = copy(probe_sums.at[:, theirs], p_land.at[0], mate)
    got_o = [copy(sums_b.at[k, :strip], land_o.at[k, :strip], mate) for k in range(2)]
    got_spill = []
    for k in range(2):
        got_s[k].wait_recv()
        spill[k] = sums_a[k, down] + land_o[k, down]
        got_spill.append(copy(spill.at[k], land_s.at[k], below))
    got_p.wait_recv()
    p_out[0] = probe_sums[:, mine] + p_land[0]
    for stage in range(len(bits) - 1):
        got_p = copy(p_out.at[stage], p_land.at[stage + 1], pairs[stage])
        if stage < 2:
            got_o[stage].wait_recv()
            fresh[stage] = sums_a[stage, :strip] + land_o[stage, :strip] + OBJECT_RELAX * own[stage]
        got_p.wait_recv()
        p_out[stage + 1] = p_out[stage] + p_land[stage + 1]
    stage = len(bits) - 1
    got_p = copy(p_out.at[stage], p_land.at[stage + 1], pairs[stage])
    got_b, got_next = [], []
    for k in range(2):
        got_spill[k].wait_recv()
        own_a[k] = (fresh[k] + land_s[k]) / weight[...]
        if not final:
            got_next.append(copy(own_a.at[k], land_na.at[k], above))
        got_b.append(copy(own_a.at[k], land_b.at[k], mate))
    got_p.wait_recv()
    total = p_out[stage] + p_land[stage + 1]
    old = probe[:, mine]
    p_new[...] = (total[:2] + relax * old) / (total[2] + relax)[None]
    got_p = copy(p_new, p_got, mate)
    probe_next[:, mine] = p_new[...]
    got_p.wait_recv()
    probe_next[:, theirs] = p_got[...]
    for k in range(2):
        got_b[k].wait_recv()
        own_b[k] = land_b[k]
    if not final:
        got_last = []
        for k in range(2):
            got_next[k].wait_recv()
            got_last.append(copy(land_na.at[k], land_nb.at[k], mate))
            next_a[k] = land_na[k]
        for k in range(2):
            got_last[k].wait_recv()
            next_b[k] = land_nb[k]
    for made in used:
        made.wait_send()


def exchange(final, relax, sums_a, sums_b, own, weight, probe_sums, probe):
    n_tile = lax.axis_size("tile")
    vmem = pl.BlockSpec(memory_space=pltpu.VMEM)
    strip_like = jax.ShapeDtypeStruct(own.shape, F32)
    outs = [strip_like] * (2 if final else 4) + [jax.ShapeDtypeStruct(probe.shape, F32)]
    stages = n_tile.bit_length() - 1
    rows = probe.shape[1] // 2
    width = probe.shape[2]
    block = pltpu.VMEM(own.shape, F32)
    return pl.pallas_call(
        lambda *refs: exchange_kernel(final, n_tile, relax, *refs),
        out_shape=outs,
        in_specs=[vmem] * 6,
        out_specs=[vmem] * len(outs),
        scratch_shapes=[
            pltpu.VMEM(sums_a.shape, F32),
            block, block, block, block, block, block,
            pltpu.VMEM((stages, 3, rows, width), F32),
            pltpu.VMEM((stages + 1, 3, rows, width), F32),
            pltpu.VMEM((2, rows, width), F32),
            pltpu.VMEM((2, rows, width), F32),
            pltpu.SemaphoreType.DMA((stages + 14,)),
            pltpu.SemaphoreType.DMA((stages + 14,)),
        ],
        compiler_params=pltpu.CompilerParams(
            collective_id=1 if final else 0, has_side_effects=True
        ),
        name="exchange",
    )(sums_a, sums_b, own, weight, probe_sums, probe)


def intro_kernel(
    n_tile, low, field, amps, listed, own_a, own_b, next_a, next_b, mate_amps, lists,
    land_na, land_nb, land_amps, land_lists, send, recv,
):
    half = own_a.shape[2]
    window = land_amps.shape[0]
    tile, core = lax.axis_index("tile"), lax.axis_index("pos")
    mate = (tile, 1 - core)
    after, before = lax.rem(tile + 1, n_tile), lax.rem(tile + n_tile - 1, n_tile)

    barrier = pltpu.get_barrier_semaphore()
    greeted = [mate, (after, core), (before, core), (after, 1 - core), (before, 1 - core)]
    for other in greeted:
        pl.semaphore_signal(barrier, inc=1, device_id=other, device_id_type=pl.DeviceIdType.MESH)
    pl.semaphore_wait(barrier, len(greeted))

    used = []

    def copy(src, dst, device):
        k = len(used)
        made = pltpu.make_async_remote_copy(
            src_ref=src, dst_ref=dst, send_sem=send.at[k], recv_sem=recv.at[k],
            device_id=device, device_id_type=pl.DeviceIdType.MESH,
        )
        used.append(made)
        made.start()
        return made

    mine = pl.ds(pl.multiple_of(core * half, half), half)
    theirs = pl.ds(pl.multiple_of((1 - core) * half, half), half)
    got_lists = [
        copy(listed, land_lists.at[0], mate),
        copy(listed, land_lists.at[1], (after, core)),
        copy(listed, land_lists.at[2], (after, 1 - core)),
    ]
    got_next = [copy(field.at[k, :, mine], land_na.at[k], (before, core)) for k in range(2)]
    got_amps = copy(amps.at[pl.ds(low, window)], land_amps, mate)
    own_a[...] = field[:, :, mine]
    own_b[...] = field[:, :, theirs]
    lists[0] = listed[...]
    for k in range(3):
        got_lists[k].wait_recv()
        lists[k + 1] = land_lists[k]
    got_amps.wait_recv()
    mate_amps[...] = land_amps[...]
    got_last = []
    for k in range(2):
        got_next[k].wait_recv()
        got_last.append(copy(land_na.at[k], land_nb.at[k], mate))
        next_a[k] = land_na[k]
    for k in range(2):
        got_last[k].wait_recv()
        next_b[k] = land_nb[k]
    for made in used:
        made.wait_send()


def intro(field, amps, listed):
    n_tile = lax.axis_size("tile")
    slot_count, patch = amps.shape[:2]
    strip, columns = field.shape[1:]
    low, window = slot_count // 4, 3 * slot_count // 8
    block = (2, strip, columns // 2)
    vmem = pl.BlockSpec(memory_space=pltpu.VMEM)
    block_like = jax.ShapeDtypeStruct(block, F32)
    taken = (window,) + amps.shape[1:]
    return pl.pallas_call(
        lambda *refs: intro_kernel(n_tile, low, *refs),
        out_shape=[block_like] * 4
        + [
            jax.ShapeDtypeStruct(taken, F32),
            jax.ShapeDtypeStruct((4,) + listed.shape, jnp.int32),
        ],
        in_specs=[vmem, pl.BlockSpec(memory_space=pl.ANY), vmem],
        out_specs=[vmem] * 6,
        scratch_shapes=[
            pltpu.VMEM(block, F32),
            pltpu.VMEM(block, F32),
            pltpu.VMEM(taken, F32),
            pltpu.VMEM((3,) + listed.shape, jnp.int32),
            pltpu.SemaphoreType.DMA((8,)),
            pltpu.SemaphoreType.DMA((8,)),
        ],
        compiler_params=pltpu.CompilerParams(collective_id=2, has_side_effects=True),
        name="intro",
    )(field, amps, listed)


def on_device(object_field, probe_field, amplitudes, scan_rows, scan_cols, live_count):
    core = lax.axis_index("pos")
    amps = amplitudes[0, 0]
    slot_count = amps.shape[0]
    strip, columns = object_field.shape[1:]
    half = columns // 2
    tables = jnp.asarray(dft_tables(probe_field.shape[1]))
    width = -(-slot_count // LANES) * LANES

    def fill(row):
        return jnp.pad(row, (0, width - row.shape[0]))

    listed = jnp.stack(
        [
            fill(scan_rows[0, 0]),
            fill(scan_cols[0, 0]),
            fill(live_count[0]),
            jnp.full((width,), core, jnp.int32),
        ]
        + [jnp.zeros((width,), jnp.int32)] * 4
    )
    own_a, own_b, next_a, next_b, mate_amps, lists = intro(object_field, amps, listed)
    probe_relax = slot_count * lax.axis_size("tile") * lax.axis_size("pos") / 4.0
    for round_number in range(ITERS):
        weight = weights(lists, probe_field, strip, half)
        sums_a, sums_b, probe_sums = visit(
            lists, probe_field, amps, mate_amps, own_a, own_b, next_a, next_b, tables
        )
        final = round_number == ITERS - 1
        results = exchange(
            final, probe_relax, sums_a, sums_b, own_a, weight, probe_sums, probe_field
        )
        if final:
            own_a, own_b, probe_field = results
        else:
            own_a, own_b, next_a, next_b, probe_field = results
    left = jnp.where(core == 0, own_a, own_b)
    right = jnp.where(core == 0, own_b, own_a)
    return (jnp.concatenate([left, right], axis=2), probe_field)


def solution(mesh):
    placed = (
        P(None, "tile", None),
        P(),
        P("tile", "pos", None, None, None),
        P("tile", "pos", None),
        P("tile", "pos", None),
        P("tile", "pos"),
    )
    return jax.shard_map(
        on_device,
        mesh=mesh,
        in_specs=placed,
        out_specs=(P(None, "tile", None), P()),
        check_vma=False,
    )
```

```python
import math

import jax
import jax.numpy as jnp
import ml_dtypes
import numpy as np
from jax import lax
from jax.experimental import pallas as pl
from jax.experimental.pallas import tpu as pltpu
from jax.sharding import PartitionSpec as P

ITERS = 2
MODULUS_FLOOR = 0.2
OBJECT_RELAX = 1.0
LANES = 128
F32 = jnp.float32
BF16 = jnp.bfloat16


def split_table(table):
    high = table.astype(ml_dtypes.bfloat16)
    low = (table - high.astype(np.float64)).astype(ml_dtypes.bfloat16)
    return high, low


def dft_tables(size):
    k = np.arange(size)
    angle = (k[:, None] * k[None, :] % size) * (2.0 * math.pi / size)
    c = np.cos(angle) / math.sqrt(size)
    s = np.sin(angle) / math.sqrt(size)
    first = np.block([[c, -s], [s, c]])
    second = np.block([[c, s], [-s, c]])
    return np.stack([*split_table(first), *split_table(second)])


def split(value):
    high = value.astype(BF16)
    low = (value - high.astype(F32)).astype(BF16)
    return high, low


def dot(a, b):
    return jnp.dot(a, b, preferred_element_type=F32)


def right_product(value, table_h, table_l):
    high, low = split(value)
    return dot(high, table_h) + (dot(low, table_h) + dot(high, table_l))


def left_product(table_h, table_l, value):
    high, low = split(value)
    return dot(table_h, high) + (dot(table_h, low) + dot(table_l, high))


def visit_kernel(
    lists, probe, amps, mate_amps, own_a, own_b, next_a, next_b, tables,
    sums_a, sums_b, probe_sums, band, acc,
):
    patch = probe.shape[1]
    half_tiles = own_a.shape[2] // LANES
    tiles = 2 * half_tiles
    strip = own_a.shape[1]
    slot_count = amps.shape[0]
    low = slot_count // 4
    own_total, mate_total = lists[0, 2, 0], lists[1, 2, 0]
    given = jnp.maximum(own_total - mate_total, 0) // 2
    kept = own_total - given
    total = kept + jnp.maximum(mate_total - own_total, 0) // 2
    base_a = lists[0, 3, 0] * half_tiles
    base_b = half_tiles - base_a
    for plane in range(2):
        for k in range(half_tiles):
            lanes = slice(k * LANES, (k + 1) * LANES)
            band[plane, base_a + k, :strip, :] = own_a[plane, :, lanes]
            band[plane, base_b + k, :strip, :] = own_b[plane, :, lanes]
            band[plane, base_a + k, strip:, :] = next_a[plane, :, lanes]
            band[plane, base_b + k, strip:, :] = next_b[plane, :, lanes]
    acc[...] = jnp.zeros_like(acc)
    probe_sums[...] = jnp.zeros_like(probe_sums)
    lane = lax.broadcasted_iota(jnp.int32, (patch, LANES), 1)

    def find(j):
        mine = j < kept
        slot = jnp.minimum(jnp.where(j < low, j, j + given), slot_count - 1)
        extra = jnp.clip(j - kept, 0, mate_amps.shape[0] - 1)
        which = jnp.where(mine, 0, 1)
        at = jnp.where(mine, slot, low + extra)
        row, col = lists[which, 0, at], lists[which, 1, at]
        q = col // LANES
        amp = jnp.where(mine, amps[slot], mate_amps[extra])
        return (row, q, lax.rem(q + 1, tiles), lax.rem(col, LANES)), amp

    def cut(place):
        r, q, q2, s = place
        back = lax.rem(LANES - s, LANES)
        parts = []
        for plane in range(2):
            left = band[plane, q, pl.ds(r, patch), :]
            right = band[plane, q2, pl.ds(r, patch), :]
            parts.append(pltpu.roll(jnp.where(lane >= s, left, right), back, 1))
        return parts

    def transform_pair(js, live, pr, pi):
        found = [find(j) for j in js]
        patches = [cut(place) for place, _ in found]
        exits = [
            jnp.concatenate([pr * a - pi * b, pr * b + pi * a], axis=1) for a, b in patches
        ]
        z = right_product(jnp.concatenate(exits, axis=0), tables[0], tables[1])
        z = jnp.concatenate(
            [
                jnp.concatenate([z[m * patch : (m + 1) * patch, c * LANES : (c + 1) * LANES] for c in range(2)], axis=0)
                for m in range(2)
            ],
            axis=1,
        )
        far = left_product(tables[2], tables[3], z)
        fr, fi = far[:patch], far[patch:]
        power = jnp.maximum(fr * fr + fi * fi, MODULUS_FLOOR * MODULUS_FLOOR)
        amp = jnp.concatenate([a * f for (_, a), f in zip(found, live)], axis=1)
        ratio = amp * lax.rsqrt(power)
        projected = jnp.concatenate([fr * ratio, fi * ratio], axis=0)
        y = left_product(tables[0], tables[1], projected)
        y = jnp.concatenate(
            [
                jnp.concatenate([y[c * patch : (c + 1) * patch, m * LANES : (m + 1) * LANES] for c in range(2)], axis=1)
                for m in range(2)
            ],
            axis=0,
        )
        back = right_product(y, tables[2], tables[3])
        backs = [
            (back[m * patch : (m + 1) * patch, :LANES], back[m * patch : (m + 1) * patch, LANES:])
            for m in range(2)
        ]
        return found, patches, backs

    def visit_pairs(first, count):
        pr, pi = probe[0], probe[1]
        pairs = []
        for member in range(count):
            js = [2 * (first + member) + m for m in range(2)]
            live = [jnp.where(j < total, 1.0, 0.0).astype(F32) for j in js]
            pairs.append(transform_pair(js, live, pr, pi) + (live,))
        for found, patches, backs, live in pairs:
            (ar, ai), (br, bi) = patches
            (ur, ui), (vr, vi) = backs
            probe_sums[0] += (ar * ur + ai * ui) + (br * vr + bi * vi)
            probe_sums[1] += (ar * ui - ai * ur) + (br * vi - bi * vr)
            probe_sums[2] += live[0] * (ar * ar + ai * ai) + live[1] * (br * br + bi * bi)
            for ((r, q, q2, s), _), (er, ei) in zip(found, backs):
                ahead = lane >= s
                for plane, term in enumerate((pr * er + pi * ei, pr * ei - pi * er)):
                    turned = pltpu.roll(term, s, 1)
                    here = acc[plane, q, pl.ds(r, patch), :]
                    there = acc[plane, q2, pl.ds(r, patch), :]
                    acc[plane, q, pl.ds(r, patch), :] = here + jnp.where(ahead, turned, 0.0)
                    acc[plane, q2, pl.ds(r, patch), :] = there + jnp.where(ahead, 0.0, turned)

    pair_total = (total + 1) // 2
    done = 0
    for count in (4, 2, 1):
        steps = (pair_total - done) // count

        def body(step, carry, done=done, count=count):
            visit_pairs(done + step * count, count)
            return carry

        lax.fori_loop(0, steps, body, 0)
        done = done + steps * count
    for plane in range(2):
        for k in range(half_tiles):
            lanes = slice(k * LANES, (k + 1) * LANES)
            sums_a[plane, :, lanes] = acc[plane, base_a + k]
            sums_b[plane, :, lanes] = acc[plane, base_b + k]


def visit(lists, probe, amps, mate_amps, own_a, own_b, next_a, next_b, tables):
    planes, strip, half = own_a.shape
    tiles = 2 * half // LANES
    smem = pl.BlockSpec(memory_space=pltpu.SMEM)
    vmem = pl.BlockSpec(memory_space=pltpu.VMEM)
    return pl.pallas_call(
        visit_kernel,
        out_shape=(
            jax.ShapeDtypeStruct((2, 2 * strip, half), F32),
            jax.ShapeDtypeStruct((2, 2 * strip, half), F32),
            jax.ShapeDtypeStruct((3,) + probe.shape[1:], F32),
        ),
        in_specs=[smem] + [vmem] * 8,
        out_specs=(vmem, vmem, vmem),
        scratch_shapes=[
            pltpu.VMEM((2, tiles, 2 * strip, LANES), F32),
            pltpu.VMEM((2, tiles, 2 * strip, LANES), F32),
        ],
        name="visit",
        cost_estimate=pl.CostEstimate(flops=10**10, bytes_accessed=10**7, transcendentals=0),
    )(lists, probe, amps, mate_amps, own_a, own_b, next_a, next_b, tables)


def weight_kernel(lists, probe, out, acc, power):
    patch = probe.shape[1]
    strip = out.shape[0]
    half_tiles = out.shape[1] // LANES
    tiles = 2 * half_tiles
    last = lists.shape[2] - 1
    base = lists[0, 3, 0] * half_tiles
    acc[...] = jnp.zeros_like(acc)
    power[...] = probe[0] * probe[0] + probe[1] * probe[1]
    lane = lax.broadcasted_iota(jnp.int32, (patch, LANES), 1)

    for group in range(4):
        down = strip if group < 2 else 0

        def add_members(first, count):
            for member in range(count):
                j = first + member
                live = j < lists[group, 2, 0]
                j = jnp.minimum(j, last)
                col = lists[group, 1, j]
                r = lists[group, 0, j] + down
                q, s = col // LANES, lax.rem(col, LANES)
                q1 = q - base
                q2 = lax.rem(q + 1, tiles) - base
                in1 = jnp.logical_and(live, jnp.logical_and(q1 >= 0, q1 < half_tiles))
                in2 = jnp.logical_and(live, jnp.logical_and(q2 >= 0, q2 < half_tiles))
                q1 = jnp.where(in1, q1, half_tiles)
                q2 = jnp.where(in2, q2, half_tiles + 1)
                turned = pltpu.roll(power[...], s, 1)
                ahead = lane >= s
                here = acc[q1, pl.ds(r, patch), :]
                there = acc[q2, pl.ds(r, patch), :]
                acc[q1, pl.ds(r, patch), :] = here + jnp.where(ahead, turned, 0.0)
                acc[q2, pl.ds(r, patch), :] = there + jnp.where(ahead, 0.0, turned)

        done = 0
        for count in (8, 2):
            steps = (lists[group, 2, 0] + (1 if count == 2 else 0) - done) // count

            def body(step, carry, done=done, count=count, add_members=add_members):
                add_members(done + step * count, count)
                return carry

            lax.fori_loop(0, steps, body, 0)
            done = done + steps * count
    for k in range(half_tiles):
        out[:, k * LANES : (k + 1) * LANES] = acc[k, strip : 2 * strip, :] + OBJECT_RELAX


def weights(lists, probe, strip, half):
    smem = pl.BlockSpec(memory_space=pltpu.SMEM)
    vmem = pl.BlockSpec(memory_space=pltpu.VMEM)
    return pl.pallas_call(
        weight_kernel,
        out_shape=jax.ShapeDtypeStruct((strip, half), F32),
        in_specs=[smem, vmem],
        out_specs=vmem,
        scratch_shapes=[
            pltpu.VMEM((half // LANES + 2, 3 * strip, LANES), F32),
            pltpu.VMEM(probe.shape[1:], F32),
        ],
        name="weights",
        cost_estimate=pl.CostEstimate(flops=10**9, bytes_accessed=10**6, transcendentals=0),
    )(lists, probe)


def exchange_kernel(
    final, n_tile, relax, sums_a, sums_b, own, weight, probe_sums, probe, *refs
):
    if final:
        own_a, own_b, probe_next = refs[:3]
        refs = refs[3:]
    else:
        own_a, own_b, next_a, next_b, probe_next = refs[:5]
        refs = refs[5:]
    land_o, spill, land_s, fresh, land_b, land_na, land_nb, p_out, p_land, p_new, p_got, send, recv = refs
    strip = own.shape[1]
    rows = p_new.shape[1]
    tile, core = lax.axis_index("tile"), lax.axis_index("pos")
    mate = (tile, 1 - core)
    below = (lax.rem(tile + 1, n_tile), core)
    above = (lax.rem(tile + n_tile - 1, n_tile), core)
    bits = [2**k for k in range(1, n_tile.bit_length() - 1)] + [1]
    pairs = [(tile + b - 2 * b * lax.rem(tile // b, 2), core) for b in bits]

    barrier = pltpu.get_barrier_semaphore()
    greeted = [mate, below, above] + pairs
    for other in greeted:
        pl.semaphore_signal(barrier, inc=1, device_id=other, device_id_type=pl.DeviceIdType.MESH)
    pl.semaphore_wait(barrier, len(greeted))

    used = []

    def copy(src, dst, device):
        k = len(used)
        made = pltpu.make_async_remote_copy(
            src_ref=src, dst_ref=dst, send_sem=send.at[k], recv_sem=recv.at[k],
            device_id=device, device_id_type=pl.DeviceIdType.MESH,
        )
        used.append(made)
        made.start()
        return made

    down = slice(strip, 2 * strip)
    mine = pl.ds(pl.multiple_of(core * rows, rows), rows)
    theirs = pl.ds(pl.multiple_of((1 - core) * rows, rows), rows)
    got_s = [copy(sums_b.at[k, down], land_o.at[k, down], mate) for k in range(2)]
    got_p = copy(probe_sums.at[:, theirs], p_land.at[0], mate)
    got_o = [copy(sums_b.at[k, :strip], land_o.at[k, :strip], mate) for k in range(2)]
    got_spill = []
    for k in range(2):
        got_s[k].wait_recv()
        spill[k] = sums_a[k, down] + land_o[k, down]
        got_spill.append(copy(spill.at[k], land_s.at[k], below))
    got_p.wait_recv()
    p_out[0] = probe_sums[:, mine] + p_land[0]
    for stage in range(len(bits) - 1):
        got_p = copy(p_out.at[stage], p_land.at[stage + 1], pairs[stage])
        if stage < 2:
            got_o[stage].wait_recv()
            fresh[stage] = sums_a[stage, :strip] + land_o[stage, :strip] + OBJECT_RELAX * own[stage]
        got_p.wait_recv()
        p_out[stage + 1] = p_out[stage] + p_land[stage + 1]
    stage = len(bits) - 1
    got_p = copy(p_out.at[stage], p_land.at[stage + 1], pairs[stage])
    got_b, got_next = [], []
    for k in range(2):
        got_spill[k].wait_recv()
        own_a[k] = (fresh[k] + land_s[k]) / weight[...]
        if not final:
            got_next.append(copy(own_a.at[k], land_na.at[k], above))
        got_b.append(copy(own_a.at[k], land_b.at[k], mate))
    got_p.wait_recv()
    total = p_out[stage] + p_land[stage + 1]
    old = probe[:, mine]
    p_new[...] = (total[:2] + relax * old) / (total[2] + relax)[None]
    got_p = copy(p_new, p_got, mate)
    probe_next[:, mine] = p_new[...]
    got_p.wait_recv()
    probe_next[:, theirs] = p_got[...]
    for k in range(2):
        got_b[k].wait_recv()
        own_b[k] = land_b[k]
    if not final:
        got_last = []
        for k in range(2):
            got_next[k].wait_recv()
            got_last.append(copy(land_na.at[k], land_nb.at[k], mate))
            next_a[k] = land_na[k]
        for k in range(2):
            got_last[k].wait_recv()
            next_b[k] = land_nb[k]
    for made in used:
        made.wait_send()


def exchange(final, relax, sums_a, sums_b, own, weight, probe_sums, probe):
    n_tile = lax.axis_size("tile")
    vmem = pl.BlockSpec(memory_space=pltpu.VMEM)
    strip_like = jax.ShapeDtypeStruct(own.shape, F32)
    outs = [strip_like] * (2 if final else 4) + [jax.ShapeDtypeStruct(probe.shape, F32)]
    stages = n_tile.bit_length() - 1
    rows = probe.shape[1] // 2
    width = probe.shape[2]
    block = pltpu.VMEM(own.shape, F32)
    return pl.pallas_call(
        lambda *refs: exchange_kernel(final, n_tile, relax, *refs),
        out_shape=outs,
        in_specs=[vmem] * 6,
        out_specs=[vmem] * len(outs),
        scratch_shapes=[
            pltpu.VMEM(sums_a.shape, F32),
            block, block, block, block, block, block,
            pltpu.VMEM((stages, 3, rows, width), F32),
            pltpu.VMEM((stages + 1, 3, rows, width), F32),
            pltpu.VMEM((2, rows, width), F32),
            pltpu.VMEM((2, rows, width), F32),
            pltpu.SemaphoreType.DMA((stages + 14,)),
            pltpu.SemaphoreType.DMA((stages + 14,)),
        ],
        compiler_params=pltpu.CompilerParams(
            collective_id=1 if final else 0, has_side_effects=True
        ),
        name="exchange",
    )(sums_a, sums_b, own, weight, probe_sums, probe)


def intro_kernel(
    n_tile, low, field, amps, listed, own_a, own_b, next_a, next_b, mate_amps, lists,
    land_na, land_nb, land_amps, land_lists, send, recv,
):
    half = own_a.shape[2]
    window = land_amps.shape[0]
    tile, core = lax.axis_index("tile"), lax.axis_index("pos")
    mate = (tile, 1 - core)
    after, before = lax.rem(tile + 1, n_tile), lax.rem(tile + n_tile - 1, n_tile)

    barrier = pltpu.get_barrier_semaphore()
    greeted = [mate, (after, core), (before, core), (after, 1 - core), (before, 1 - core)]
    for other in greeted:
        pl.semaphore_signal(barrier, inc=1, device_id=other, device_id_type=pl.DeviceIdType.MESH)
    pl.semaphore_wait(barrier, len(greeted))

    used = []

    def copy(src, dst, device):
        k = len(used)
        made = pltpu.make_async_remote_copy(
            src_ref=src, dst_ref=dst, send_sem=send.at[k], recv_sem=recv.at[k],
            device_id=device, device_id_type=pl.DeviceIdType.MESH,
        )
        used.append(made)
        made.start()
        return made

    mine = pl.ds(pl.multiple_of(core * half, half), half)
    theirs = pl.ds(pl.multiple_of((1 - core) * half, half), half)
    got_lists = [
        copy(listed, land_lists.at[0], mate),
        copy(listed, land_lists.at[1], (after, core)),
        copy(listed, land_lists.at[2], (after, 1 - core)),
    ]
    got_next = [copy(field.at[k, :, mine], land_na.at[k], (before, core)) for k in range(2)]
    got_amps = copy(amps.at[pl.ds(low, window)], land_amps, mate)
    own_a[...] = field[:, :, mine]
    own_b[...] = field[:, :, theirs]
    lists[0] = listed[...]
    for k in range(3):
        got_lists[k].wait_recv()
        lists[k + 1] = land_lists[k]
    got_amps.wait_recv()
    mate_amps[...] = land_amps[...]
    got_last = []
    for k in range(2):
        got_next[k].wait_recv()
        got_last.append(copy(land_na.at[k], land_nb.at[k], mate))
        next_a[k] = land_na[k]
    for k in range(2):
        got_last[k].wait_recv()
        next_b[k] = land_nb[k]
    for made in used:
        made.wait_send()


def intro(field, amps, listed):
    n_tile = lax.axis_size("tile")
    slot_count, patch = amps.shape[:2]
    strip, columns = field.shape[1:]
    low, window = slot_count // 4, 3 * slot_count // 8
    block = (2, strip, columns // 2)
    vmem = pl.BlockSpec(memory_space=pltpu.VMEM)
    block_like = jax.ShapeDtypeStruct(block, F32)
    taken = (window,) + amps.shape[1:]
    return pl.pallas_call(
        lambda *refs: intro_kernel(n_tile, low, *refs),
        out_shape=[block_like] * 4
        + [
            jax.ShapeDtypeStruct(taken, F32),
            jax.ShapeDtypeStruct((4,) + listed.shape, jnp.int32),
        ],
        in_specs=[vmem, pl.BlockSpec(memory_space=pl.ANY), vmem],
        out_specs=[vmem] * 6,
        scratch_shapes=[
            pltpu.VMEM(block, F32),
            pltpu.VMEM(block, F32),
            pltpu.VMEM(taken, F32),
            pltpu.VMEM((3,) + listed.shape, jnp.int32),
            pltpu.SemaphoreType.DMA((8,)),
            pltpu.SemaphoreType.DMA((8,)),
        ],
        compiler_params=pltpu.CompilerParams(collective_id=2, has_side_effects=True),
        name="intro",
    )(field, amps, listed)


def on_device(object_field, probe_field, amplitudes, scan_rows, scan_cols, live_count):
    core = lax.axis_index("pos")
    amps = amplitudes[0, 0]
    slot_count = amps.shape[0]
    strip, columns = object_field.shape[1:]
    half = columns // 2
    tables = jnp.asarray(dft_tables(probe_field.shape[1]))
    width = -(-slot_count // LANES) * LANES

    def fill(row):
        return jnp.pad(row, (0, width - row.shape[0]))

    listed = jnp.stack(
        [
            fill(scan_rows[0, 0]),
            fill(scan_cols[0, 0]),
            fill(live_count[0]),
            jnp.full((width,), core, jnp.int32),
        ]
        + [jnp.zeros((width,), jnp.int32)] * 4
    )
    own_a, own_b, next_a, next_b, mate_amps, lists = intro(object_field, amps, listed)
    probe_relax = slot_count * lax.axis_size("tile") * lax.axis_size("pos") / 4.0
    for round_number in range(ITERS):
        weight = weights(lists, probe_field, strip, half)
        sums_a, sums_b, probe_sums = visit(
            lists, probe_field, amps, mate_amps, own_a, own_b, next_a, next_b, tables
        )
        final = round_number == ITERS - 1
        results = exchange(
            final, probe_relax, sums_a, sums_b, own_a, weight, probe_sums, probe_field
        )
        if final:
            own_a, own_b, probe_field = results
        else:
            own_a, own_b, next_a, next_b, probe_field = results
    left = jnp.where(core == 0, own_a, own_b)
    right = jnp.where(core == 0, own_b, own_a)
    return (jnp.concatenate([left, right], axis=2), probe_field)


def solution(mesh):
    placed = (
        P(None, "tile", None),
        P(),
        P("tile", "pos", None, None, None),
        P("tile", "pos", None),
        P("tile", "pos", None),
        P("tile", "pos"),
    )
    return jax.shard_map(
        on_device,
        mesh=mesh,
        in_specs=placed,
        out_specs=(P(None, "tile", None), P()),
        check_vma=False,
    )
```

```python
import math

import jax
import jax.numpy as jnp
import ml_dtypes
import numpy as np
from jax import lax
from jax.experimental import pallas as pl
from jax.experimental.pallas import tpu as pltpu
from jax.sharding import PartitionSpec as P

ITERS = 2
MODULUS_FLOOR = 0.2
OBJECT_RELAX = 1.0
LANES = 128
F32 = jnp.float32
BF16 = jnp.bfloat16


def split_table(table):
    high = table.astype(ml_dtypes.bfloat16)
    low = (table - high.astype(np.float64)).astype(ml_dtypes.bfloat16)
    return high, low


def dft_tables(size):
    k = np.arange(size)
    angle = (k[:, None] * k[None, :] % size) * (2.0 * math.pi / size)
    c = np.cos(angle) / math.sqrt(size)
    s = np.sin(angle) / math.sqrt(size)
    first = np.block([[c, -s], [s, c]])
    second = np.block([[c, s], [-s, c]])
    return np.stack([*split_table(first), *split_table(second)])


def split(value):
    high = value.astype(BF16)
    low = (value - high.astype(F32)).astype(BF16)
    return high, low


def dot(a, b):
    return jnp.dot(a, b, preferred_element_type=F32)


def right_product(value, table_h, table_l):
    high, low = split(value)
    return dot(high, table_h) + (dot(low, table_h) + dot(high, table_l))


def left_product(table_h, table_l, value):
    high, low = split(value)
    return dot(table_h, high) + (dot(table_h, low) + dot(table_l, high))


def visit_kernel(
    lists, probe, amps, mate_amps, own_a, own_b, next_a, next_b, tables,
    sums_a, sums_b, probe_sums, band, acc,
):
    patch = probe.shape[1]
    half_tiles = own_a.shape[2] // LANES
    tiles = 2 * half_tiles
    strip = own_a.shape[1]
    slot_count = amps.shape[0]
    low = slot_count // 4
    own_total, mate_total = lists[0, 2, 0], lists[1, 2, 0]
    given = jnp.maximum(own_total - mate_total, 0) // 2
    kept = own_total - given
    total = kept + jnp.maximum(mate_total - own_total, 0) // 2
    base_a = lists[0, 3, 0] * half_tiles
    base_b = half_tiles - base_a
    for plane in range(2):
        for k in range(half_tiles):
            lanes = slice(k * LANES, (k + 1) * LANES)
            band[plane, base_a + k, :strip, :] = own_a[plane, :, lanes]
            band[plane, base_b + k, :strip, :] = own_b[plane, :, lanes]
            band[plane, base_a + k, strip:, :] = next_a[plane, :, lanes]
            band[plane, base_b + k, strip:, :] = next_b[plane, :, lanes]
    acc[...] = jnp.zeros_like(acc)
    probe_sums[...] = jnp.zeros_like(probe_sums)
    lane = lax.broadcasted_iota(jnp.int32, (patch, LANES), 1)

    def find(j):
        mine = j < kept
        slot = jnp.minimum(jnp.where(j < low, j, j + given), slot_count - 1)
        extra = jnp.clip(j - kept, 0, mate_amps.shape[0] - 1)
        which = jnp.where(mine, 0, 1)
        at = jnp.where(mine, slot, low + extra)
        row, col = lists[which, 0, at], lists[which, 1, at]
        q = col // LANES
        amp = jnp.where(mine, amps[slot], mate_amps[extra])
        return (row, q, lax.rem(q + 1, tiles), lax.rem(col, LANES)), amp

    def cut(place):
        r, q, q2, s = place
        back = lax.rem(LANES - s, LANES)
        parts = []
        for plane in range(2):
            left = band[plane, q, pl.ds(r, patch), :]
            right = band[plane, q2, pl.ds(r, patch), :]
            parts.append(pltpu.roll(jnp.where(lane >= s, left, right), back, 1))
        return parts

    def transform_pair(js, live, pr, pi):
        found = [find(j) for j in js]
        patches = [cut(place) for place, _ in found]
        exits = [
            jnp.concatenate([pr * a - pi * b, pr * b + pi * a], axis=1) for a, b in patches
        ]
        z = right_product(jnp.concatenate(exits, axis=0), tables[0], tables[1])
        z = jnp.concatenate(
            [
                jnp.concatenate([z[m * patch : (m + 1) * patch, c * LANES : (c + 1) * LANES] for c in range(2)], axis=0)
                for m in range(2)
            ],
            axis=1,
        )
        far = left_product(tables[2], tables[3], z)
        fr, fi = far[:patch], far[patch:]
        power = jnp.maximum(fr * fr + fi * fi, MODULUS_FLOOR * MODULUS_FLOOR)
        amp = jnp.concatenate([a * f for (_, a), f in zip(found, live)], axis=1)
        ratio = amp * lax.rsqrt(power)
        projected = jnp.concatenate([fr * ratio, fi * ratio], axis=0)
        y = left_product(tables[0], tables[1], projected)
        y = jnp.concatenate(
            [
                jnp.concatenate([y[c * patch : (c + 1) * patch, m * LANES : (m + 1) * LANES] for c in range(2)], axis=1)
                for m in range(2)
            ],
            axis=0,
        )
        back = right_product(y, tables[2], tables[3])
        backs = [
            (back[m * patch : (m + 1) * patch, :LANES], back[m * patch : (m + 1) * patch, LANES:])
            for m in range(2)
        ]
        return found, patches, backs

    def visit_pairs(first, count):
        pr, pi = probe[0], probe[1]
        pairs = []
        for member in range(count):
            js = [2 * (first + member) + m for m in range(2)]
            live = [jnp.where(j < total, 1.0, 0.0).astype(F32) for j in js]
            pairs.append(transform_pair(js, live, pr, pi) + (live,))
        for found, patches, backs, live in pairs:
            (ar, ai), (br, bi) = patches
            (ur, ui), (vr, vi) = backs
            probe_sums[0] += (ar * ur + ai * ui) + (br * vr + bi * vi)
            probe_sums[1] += (ar * ui - ai * ur) + (br * vi - bi * vr)
            probe_sums[2] += live[0] * (ar * ar + ai * ai) + live[1] * (br * br + bi * bi)
            for ((r, q, q2, s), _), (er, ei) in zip(found, backs):
                ahead = lane >= s
                for plane, term in enumerate((pr * er + pi * ei, pr * ei - pi * er)):
                    turned = pltpu.roll(term, s, 1)
                    here = acc[plane, q, pl.ds(r, patch), :]
                    there = acc[plane, q2, pl.ds(r, patch), :]
                    acc[plane, q, pl.ds(r, patch), :] = here + jnp.where(ahead, turned, 0.0)
                    acc[plane, q2, pl.ds(r, patch), :] = there + jnp.where(ahead, 0.0, turned)

    pair_total = (total + 1) // 2
    done = 0
    for count in (4, 2, 1):
        steps = (pair_total - done) // count

        def body(step, carry, done=done, count=count):
            visit_pairs(done + step * count, count)
            return carry

        lax.fori_loop(0, steps, body, 0)
        done = done + steps * count
    for plane in range(2):
        for k in range(half_tiles):
            lanes = slice(k * LANES, (k + 1) * LANES)
            sums_a[plane, :, lanes] = acc[plane, base_a + k]
            sums_b[plane, :, lanes] = acc[plane, base_b + k]


def visit(lists, probe, amps, mate_amps, own_a, own_b, next_a, next_b, tables):
    planes, strip, half = own_a.shape
    tiles = 2 * half // LANES
    smem = pl.BlockSpec(memory_space=pltpu.SMEM)
    vmem = pl.BlockSpec(memory_space=pltpu.VMEM)
    return pl.pallas_call(
        visit_kernel,
        out_shape=(
            jax.ShapeDtypeStruct((2, 2 * strip, half), F32),
            jax.ShapeDtypeStruct((2, 2 * strip, half), F32),
            jax.ShapeDtypeStruct((3,) + probe.shape[1:], F32),
        ),
        in_specs=[smem] + [vmem] * 8,
        out_specs=(vmem, vmem, vmem),
        scratch_shapes=[
            pltpu.VMEM((2, tiles, 2 * strip, LANES), F32),
            pltpu.VMEM((2, tiles, 2 * strip, LANES), F32),
        ],
        name="visit",
        cost_estimate=pl.CostEstimate(flops=10**10, bytes_accessed=10**7, transcendentals=0),
    )(lists, probe, amps, mate_amps, own_a, own_b, next_a, next_b, tables)


def weight_kernel(lists, probe, out, acc, power):
    patch = probe.shape[1]
    strip = out.shape[0]
    half_tiles = out.shape[1] // LANES
    tiles = 2 * half_tiles
    last = lists.shape[2] - 1
    base = lists[0, 3, 0] * half_tiles
    acc[...] = jnp.zeros_like(acc)
    power[...] = probe[0] * probe[0] + probe[1] * probe[1]
    lane = lax.broadcasted_iota(jnp.int32, (patch, LANES), 1)

    for group in range(4):
        down = strip if group < 2 else 0

        def add_members(first, count):
            for member in range(count):
                j = first + member
                live = j < lists[group, 2, 0]
                j = jnp.minimum(j, last)
                col = lists[group, 1, j]
                r = lists[group, 0, j] + down
                q, s = col // LANES, lax.rem(col, LANES)
                q1 = q - base
                q2 = lax.rem(q + 1, tiles) - base
                in1 = jnp.logical_and(live, jnp.logical_and(q1 >= 0, q1 < half_tiles))
                in2 = jnp.logical_and(live, jnp.logical_and(q2 >= 0, q2 < half_tiles))
                q1 = jnp.where(in1, q1, half_tiles)
                q2 = jnp.where(in2, q2, half_tiles + 1)
                turned = pltpu.roll(power[...], s, 1)
                ahead = lane >= s
                here = acc[q1, pl.ds(r, patch), :]
                there = acc[q2, pl.ds(r, patch), :]
                acc[q1, pl.ds(r, patch), :] = here + jnp.where(ahead, turned, 0.0)
                acc[q2, pl.ds(r, patch), :] = there + jnp.where(ahead, 0.0, turned)

        done = 0
        for count in (8, 2):
            steps = (lists[group, 2, 0] + (1 if count == 2 else 0) - done) // count

            def body(step, carry, done=done, count=count, add_members=add_members):
                add_members(done + step * count, count)
                return carry

            lax.fori_loop(0, steps, body, 0)
            done = done + steps * count
    for k in range(half_tiles):
        out[:, k * LANES : (k + 1) * LANES] = acc[k, strip : 2 * strip, :] + OBJECT_RELAX


def weights(lists, probe, strip, half):
    smem = pl.BlockSpec(memory_space=pltpu.SMEM)
    vmem = pl.BlockSpec(memory_space=pltpu.VMEM)
    return pl.pallas_call(
        weight_kernel,
        out_shape=jax.ShapeDtypeStruct((strip, half), F32),
        in_specs=[smem, vmem],
        out_specs=vmem,
        scratch_shapes=[
            pltpu.VMEM((half // LANES + 2, 3 * strip, LANES), F32),
            pltpu.VMEM(probe.shape[1:], F32),
        ],
        name="weights",
        cost_estimate=pl.CostEstimate(flops=10**9, bytes_accessed=10**6, transcendentals=0),
    )(lists, probe)


def exchange_kernel(
    final, n_tile, relax, sums_a, sums_b, own, weight, probe_sums, probe, *refs
):
    if final:
        own_a, own_b, probe_next = refs[:3]
        refs = refs[3:]
    else:
        own_a, own_b, next_a, next_b, probe_next = refs[:5]
        refs = refs[5:]
    land_o, spill, land_s, fresh, land_b, land_na, land_nb, p_out, p_land, p_new, p_got, send, recv = refs
    strip = own.shape[1]
    rows = p_new.shape[1]
    tile, core = lax.axis_index("tile"), lax.axis_index("pos")
    mate = (tile, 1 - core)
    below = (lax.rem(tile + 1, n_tile), core)
    above = (lax.rem(tile + n_tile - 1, n_tile), core)
    bits = [2**k for k in range(1, n_tile.bit_length() - 1)] + [1]
    pairs = [(tile + b - 2 * b * lax.rem(tile // b, 2), core) for b in bits]

    barrier = pltpu.get_barrier_semaphore()
    greeted = [mate, below, above] + pairs
    for other in greeted:
        pl.semaphore_signal(barrier, inc=1, device_id=other, device_id_type=pl.DeviceIdType.MESH)
    pl.semaphore_wait(barrier, len(greeted))

    used = []

    def copy(src, dst, device):
        k = len(used)
        made = pltpu.make_async_remote_copy(
            src_ref=src, dst_ref=dst, send_sem=send.at[k], recv_sem=recv.at[k],
            device_id=device, device_id_type=pl.DeviceIdType.MESH,
        )
        used.append(made)
        made.start()
        return made

    mine = pl.ds(pl.multiple_of(core * rows, rows), rows)
    theirs = pl.ds(pl.multiple_of((1 - core) * rows, rows), rows)
    part = strip // 2
    chunks = [(k, lo, lo + part) for k in range(2) for lo in (0, part)]
    got_s = [
        copy(sums_b.at[k, strip + lo : strip + hi], land_o.at[k, strip + lo : strip + hi], mate)
        for k, lo, hi in chunks
    ]
    got_p = copy(probe_sums.at[:, theirs], p_land.at[0], mate)
    got_o = [copy(sums_b.at[k, :strip], land_o.at[k, :strip], mate) for k in range(2)]
    got_spill = []
    for got, (k, lo, hi) in zip(got_s, chunks):
        got.wait_recv()
        spill[k, lo:hi] = (
            sums_a[k, strip + lo : strip + hi] + land_o[k, strip + lo : strip + hi]
        )
        got_spill.append(copy(spill.at[k, lo:hi], land_s.at[k, lo:hi], below))
    got_p.wait_recv()
    p_out[0] = probe_sums[:, mine] + p_land[0]
    got_p = copy(p_out.at[0], p_land.at[1], pairs[0])
    for k in range(2):
        got_o[k].wait_recv()
        fresh[k] = sums_a[k, :strip] + land_o[k, :strip] + OBJECT_RELAX * own[k]
    got_b, got_next = [], []
    stages = len(bits)
    for step in range(max(len(chunks), stages - 1)):
        if step < len(chunks):
            k, lo, hi = chunks[step]
            got_spill[step].wait_recv()
            own_a[k, lo:hi] = (fresh[k, lo:hi] + land_s[k, lo:hi]) / weight[lo:hi]
            if not final:
                got_next.append(copy(own_a.at[k, lo:hi], land_na.at[k, lo:hi], above))
            got_b.append(copy(own_a.at[k, lo:hi], land_b.at[k, lo:hi], mate))
        if step < stages - 1:
            got_p.wait_recv()
            p_out[step + 1] = p_out[step] + p_land[step + 1]
            got_p = copy(p_out.at[step + 1], p_land.at[step + 2], pairs[step + 1])
    got_p.wait_recv()
    total = p_out[stages - 1] + p_land[stages]
    old = probe[:, mine]
    p_new[...] = (total[:2] + relax * old) / (total[2] + relax)[None]
    got_p = copy(p_new, p_got, mate)
    probe_next[:, mine] = p_new[...]
    got_p.wait_recv()
    probe_next[:, theirs] = p_got[...]
    for got, (k, lo, hi) in zip(got_b, chunks):
        got.wait_recv()
        own_b[k, lo:hi] = land_b[k, lo:hi]
    if not final:
        got_last = []
        for got, (k, lo, hi) in zip(got_next, chunks):
            got.wait_recv()
            got_last.append(copy(land_na.at[k, lo:hi], land_nb.at[k, lo:hi], mate))
            next_a[k, lo:hi] = land_na[k, lo:hi]
        for got, (k, lo, hi) in zip(got_last, chunks):
            got.wait_recv()
            next_b[k, lo:hi] = land_nb[k, lo:hi]
    for made in used:
        made.wait_send()


def exchange(final, relax, sums_a, sums_b, own, weight, probe_sums, probe):
    n_tile = lax.axis_size("tile")
    vmem = pl.BlockSpec(memory_space=pltpu.VMEM)
    strip_like = jax.ShapeDtypeStruct(own.shape, F32)
    outs = [strip_like] * (2 if final else 4) + [jax.ShapeDtypeStruct(probe.shape, F32)]
    stages = n_tile.bit_length() - 1
    rows = probe.shape[1] // 2
    width = probe.shape[2]
    block = pltpu.VMEM(own.shape, F32)
    return pl.pallas_call(
        lambda *refs: exchange_kernel(final, n_tile, relax, *refs),
        out_shape=outs,
        in_specs=[vmem] * 6,
        out_specs=[vmem] * len(outs),
        scratch_shapes=[
            pltpu.VMEM(sums_a.shape, F32),
            block, block, block, block, block, block,
            pltpu.VMEM((stages, 3, rows, width), F32),
            pltpu.VMEM((stages + 1, 3, rows, width), F32),
            pltpu.VMEM((2, rows, width), F32),
            pltpu.VMEM((2, rows, width), F32),
            pltpu.SemaphoreType.DMA((stages + 24,)),
            pltpu.SemaphoreType.DMA((stages + 24,)),
        ],
        compiler_params=pltpu.CompilerParams(
            collective_id=1 if final else 0, has_side_effects=True
        ),
        name="exchange",
    )(sums_a, sums_b, own, weight, probe_sums, probe)


def intro_kernel(
    n_tile, low, field, amps, listed, own_a, own_b, next_a, next_b, mate_amps, lists,
    land_na, land_nb, land_amps, land_lists, send, recv,
):
    half = own_a.shape[2]
    window = land_amps.shape[0]
    tile, core = lax.axis_index("tile"), lax.axis_index("pos")
    mate = (tile, 1 - core)
    after, before = lax.rem(tile + 1, n_tile), lax.rem(tile + n_tile - 1, n_tile)

    barrier = pltpu.get_barrier_semaphore()
    greeted = [mate, (after, core), (before, core), (after, 1 - core), (before, 1 - core)]
    for other in greeted:
        pl.semaphore_signal(barrier, inc=1, device_id=other, device_id_type=pl.DeviceIdType.MESH)
    pl.semaphore_wait(barrier, len(greeted))

    used = []

    def copy(src, dst, device):
        k = len(used)
        made = pltpu.make_async_remote_copy(
            src_ref=src, dst_ref=dst, send_sem=send.at[k], recv_sem=recv.at[k],
            device_id=device, device_id_type=pl.DeviceIdType.MESH,
        )
        used.append(made)
        made.start()
        return made

    mine = pl.ds(pl.multiple_of(core * half, half), half)
    theirs = pl.ds(pl.multiple_of((1 - core) * half, half), half)
    got_lists = [
        copy(listed, land_lists.at[0], mate),
        copy(listed, land_lists.at[1], (after, core)),
        copy(listed, land_lists.at[2], (after, 1 - core)),
    ]
    got_next = [copy(field.at[k, :, mine], land_na.at[k], (before, core)) for k in range(2)]
    got_amps = copy(amps.at[pl.ds(low, window)], land_amps, mate)
    own_a[...] = field[:, :, mine]
    own_b[...] = field[:, :, theirs]
    lists[0] = listed[...]
    for k in range(3):
        got_lists[k].wait_recv()
        lists[k + 1] = land_lists[k]
    got_amps.wait_recv()
    mate_amps[...] = land_amps[...]
    got_last = []
    for k in range(2):
        got_next[k].wait_recv()
        got_last.append(copy(land_na.at[k], land_nb.at[k], mate))
        next_a[k] = land_na[k]
    for k in range(2):
        got_last[k].wait_recv()
        next_b[k] = land_nb[k]
    for made in used:
        made.wait_send()


def intro(field, amps, listed):
    n_tile = lax.axis_size("tile")
    slot_count, patch = amps.shape[:2]
    strip, columns = field.shape[1:]
    low, window = slot_count // 4, 3 * slot_count // 8
    block = (2, strip, columns // 2)
    vmem = pl.BlockSpec(memory_space=pltpu.VMEM)
    block_like = jax.ShapeDtypeStruct(block, F32)
    taken = (window,) + amps.shape[1:]
    return pl.pallas_call(
        lambda *refs: intro_kernel(n_tile, low, *refs),
        out_shape=[block_like] * 4
        + [
            jax.ShapeDtypeStruct(taken, F32),
            jax.ShapeDtypeStruct((4,) + listed.shape, jnp.int32),
        ],
        in_specs=[vmem, pl.BlockSpec(memory_space=pl.ANY), vmem],
        out_specs=[vmem] * 6,
        scratch_shapes=[
            pltpu.VMEM(block, F32),
            pltpu.VMEM(block, F32),
            pltpu.VMEM(taken, F32),
            pltpu.VMEM((3,) + listed.shape, jnp.int32),
            pltpu.SemaphoreType.DMA((8,)),
            pltpu.SemaphoreType.DMA((8,)),
        ],
        compiler_params=pltpu.CompilerParams(collective_id=2, has_side_effects=True),
        name="intro",
    )(field, amps, listed)


def on_device(object_field, probe_field, amplitudes, scan_rows, scan_cols, live_count):
    core = lax.axis_index("pos")
    amps = amplitudes[0, 0]
    slot_count = amps.shape[0]
    strip, columns = object_field.shape[1:]
    half = columns // 2
    tables = jnp.asarray(dft_tables(probe_field.shape[1]))
    width = -(-slot_count // LANES) * LANES

    def fill(row):
        return jnp.pad(row, (0, width - row.shape[0]))

    listed = jnp.stack(
        [
            fill(scan_rows[0, 0]),
            fill(scan_cols[0, 0]),
            fill(live_count[0]),
            jnp.full((width,), core, jnp.int32),
        ]
        + [jnp.zeros((width,), jnp.int32)] * 4
    )
    own_a, own_b, next_a, next_b, mate_amps, lists = intro(object_field, amps, listed)
    probe_relax = slot_count * lax.axis_size("tile") * lax.axis_size("pos") / 4.0
    for round_number in range(ITERS):
        weight = weights(lists, probe_field, strip, half)
        sums_a, sums_b, probe_sums = visit(
            lists, probe_field, amps, mate_amps, own_a, own_b, next_a, next_b, tables
        )
        final = round_number == ITERS - 1
        results = exchange(
            final, probe_relax, sums_a, sums_b, own_a, weight, probe_sums, probe_field
        )
        if final:
            own_a, own_b, probe_field = results
        else:
            own_a, own_b, next_a, next_b, probe_field = results
    left = jnp.where(core == 0, own_a, own_b)
    right = jnp.where(core == 0, own_b, own_a)
    return (jnp.concatenate([left, right], axis=2), probe_field)


def solution(mesh):
    placed = (
        P(None, "tile", None),
        P(),
        P("tile", "pos", None, None, None),
        P("tile", "pos", None),
        P("tile", "pos", None),
        P("tile", "pos"),
    )
    return jax.shard_map(
        on_device,
        mesh=mesh,
        in_specs=placed,
        out_specs=(P(None, "tile", None), P()),
        check_vma=False,
    )
```
